768 devices in a mesh: blk: 384 (over z, x, y_hi, core), nrm: 2 (over y_lo).
Axes of the slice: x: 4, y: 8 (y_hi: 4, y_lo: 2; y = y_hi * 2 + y_lo), z: 12, core: 2. Of those that a mesh axis runs over, the one named last changes fastest.
Arguments:
- right_side: float32 [10, 3072, 512], P(None, 'blk', 'nrm'), may hold values from -6 to 6
- mean_flow: float32 [5, 3072, 512], P(None, 'blk', 'nrm'), may hold values from -4 to 4
- jac_basis: float32 [4, 5, 10, 10], replicated, may hold values from -0.23 to 0.23
- pattern: int32 [4, 3072, 512], P(None, 'blk', 'nrm'), may hold values 0 or 1
- shift_diag: float32 [3072, 512], P('blk', 'nrm'), may hold values from 1.2 to 2.4
- dissipation: float32 [3072, 512], P('blk', 'nrm'), may hold values from 0.04 to 0.15
- donors: int32 [384, 2, 512], P('blk', None, 'nrm'), may hold values from 0 to 511, as said below
Outputs:
- solution: float32 [10, 3072, 512], P(None, 'blk', 'nrm')
- residual: float32 [10, 3072, 512], P(None, 'blk', 'nrm')
The draws below stay inside these ranges and needn't reach their ends.
Inputs may be any that keep to these rules, and one draw needn't show every extreme that they name: donors[b, s, j] lies in the same slab of 256 wall-normal cells as j (the same value of j // 256) and differs from j by at most 3.
All inputs are finite; a program needn't handle non-finite values. No bound on the sum of `pattern` on one device may be relied on, other than what follows from the above.
Results may differ from the reference program's by a relative error of at most 0.00015.
Values sent between devices are 32-bit elements; how exact they have to be, the bound alone decides.
No kernel may reach another device: no remote copies, remote signals or barrier semaphores. Data moves between devices by JAX's collectives and lax.ppermute only.
A program may use at most 32 MiB of HBM per device.

```python
import math
import jax
import jax.numpy as jnp
from jax import lax

NVAR = 10
NMEAN = 5
CI = 8
CJ = 256
ITERS = 6
BLOCKS = 384
NI = 3072
NJ = 512
N_BLK = 384


def draw_donors(key, part):
    base = jnp.arange(NJ, dtype=jnp.int32)
    offset = jax.random.randint(key, (BLOCKS, 2, NJ), -3, 4, dtype=jnp.int32)
    local = base % CJ
    slab = base - local
    return (slab + jnp.clip(local + offset, 0, CJ - 1)).astype(jnp.int32)


def draw_jac_basis(key, part):
    scales = jnp.array([0.018, 0.018, 0.045, 0.045], jnp.float32).reshape(4, 1, 1, 1)
    base = jax.random.truncated_normal(key, -5.0, 5.0, (4, NMEAN, NVAR, NVAR), jnp.float32)
    return (base * scales).astype(jnp.float32)


def with_ends(drawn, stream_key, least, top_value):
    dims = drawn.shape
    index_at = [jax.random.randint(jax.random.fold_in(stream_key, axis), (), 0, dims[axis]) for axis in range(len(dims))]
    drawn = drawn.at[tuple(index_at)].set(least)
    longest = dims.index(max(dims))
    index_at[longest] = (index_at[longest] + 1) % dims[longest]
    return drawn.at[tuple(index_at)].set(top_value)


def levels(stream_key, shape, shards, least, high):
    def one(position, shards_of):
        draws = jax.random.uniform(jax.random.fold_in(jax.random.fold_in(stream_key, 6), position), (shards_of,), jnp.float32, least / len(shards), high / len(shards))
        return jnp.repeat(jnp.exp(draws), shape[position] // shards_of).reshape((-1,) + (1,) * (len(shape) - position - 1))

    gain = one(*shards[0])
    for cut in shards[1:]:
        gain = gain * one(*cut)
    return gain


def gaussian(key, shape, width, reach, pieces=(), kind=jnp.bfloat16):
    values = jax.random.normal(key, shape, jnp.float32) * width
    if len(pieces) > 0:
        values = levels(key, shape, pieces, -0.22, 0.18) * values
    return jnp.clip(values, min=-reach, max=reach).astype(kind)


def setup_inputs(seed: int = 0) -> dict:
    streams_of = jax.random.split(jax.random.key(seed), 8)
    right_side = gaussian(streams_of[0], (NVAR, NI, NJ), 1.0, 6.0, ((1, 384), (2, 2)), jnp.float32)
    mean_flow = gaussian(streams_of[1], (NMEAN, NI, NJ), 1.0, 4.0, ((1, 384), (2, 2)), jnp.float32)
    jac_basis = draw_jac_basis(jax.random.fold_in(streams_of[7], 71), 0)
    pattern = with_ends((jax.random.randint(streams_of[3], (4, NI, NJ), 0, 8) < 7).astype(jnp.int32), jax.random.fold_in(streams_of[3], 1), 0, 1)
    shift_diag = jnp.clip(jnp.exp(math.log(2.4) - 0.6931472 * jax.random.uniform(streams_of[4], (NI, NJ), jnp.float32) ** levels(streams_of[4], (NI, NJ), ((0, 384), (1, 2)), -0.2, 0.2)), 1.2, 2.4)
    dissipation = jnp.clip(jnp.exp(math.log(0.15) - 1.3217559 * jax.random.uniform(streams_of[5], (NI, NJ), jnp.float32) ** levels(streams_of[5], (NI, NJ), ((0, 384), (1, 2)), -0.2, 0.2)), 0.04, 0.15)
    donors = draw_donors(jax.random.fold_in(streams_of[7], 71), 0)
    return dict(right_side=right_side, mean_flow=mean_flow, jac_basis=jac_basis, pattern=pattern, shift_diag=shift_diag, dissipation=dissipation, donors=donors)


OMEGA = 0.3
DELTA = 0.9


def rotate(v):
    half = v.shape[0] // 2
    return jnp.concatenate([-v[half:], v[:half]], 0)


def reference(right_side, mean_flow, jac_basis, pattern, shift_diag, dissipation, donors):
    highest = lax.Precision.HIGHEST

    def blocks(a):
        return a.reshape(a.shape[0], N_BLK, CI, NJ)

    flow = blocks(mean_flow)
    masks = blocks(pattern).astype(jnp.float32)
    shifts = shift_diag.reshape(N_BLK, CI, NJ)
    damping = dissipation.reshape(N_BLK, CI, NJ)
    left_index = jnp.broadcast_to(donors[None, :, 0, None, :], (NVAR, N_BLK, 2, NJ)).astype(jnp.int32)
    right_index = jnp.broadcast_to(donors[None, :, 1, None, :], (NVAR, N_BLK, 2, NJ)).astype(jnp.int32)

    def apply_op(vec):
        v4 = blocks(vec)
        zero = jnp.zeros((NVAR, 1, 2, NJ), jnp.float32)
        left = jnp.concatenate([zero, v4[:, :-1, CI - 2:, :]], 1)
        right = jnp.concatenate([v4[:, 1:, :2, :], zero], 1)
        left = jnp.take_along_axis(left, left_index, axis=3)
        right = jnp.take_along_axis(right, right_index, axis=3)
        wide = jnp.concatenate([left, v4, right], 2)
        tall = jnp.pad(v4, ((0, 0), (0, 0), (0, 0), (1, 1)))
        neighbours = [wide[:, :, 1:CI + 1], wide[:, :, 3:CI + 3], tall[..., :-2], tall[..., 2:]]
        result = shifts * v4 + OMEGA * rotate(v4) + damping * (wide[:, :, 0:CI] + wide[:, :, 4:CI + 4])
        for face in range(4):
            term = jnp.zeros_like(v4)
            for comp in range(NMEAN):
                term = term + flow[comp] * jnp.einsum("ab,bxyz->axyz", jac_basis[face, comp], neighbours[face], precision=highest)
            result = result + masks[face] * term
        return result.reshape(NVAR, NI, NJ)

    def precond(vec):
        return (shift_diag * vec - OMEGA * rotate(vec)) / (shift_diag * shift_diag + OMEGA * OMEGA)

    sigma = 1.0 / DELTA
    rho = DELTA
    solution = jnp.zeros_like(right_side)
    residual = right_side
    direction = precond(residual)
    for step in range(ITERS):
        solution = solution + direction
        residual = residual - apply_op(direction)
        if step + 1 < ITERS:
            rho_new = 1.0 / (2.0 * sigma - rho)
            direction = rho_new * rho * direction + (2.0 * rho_new / DELTA) * precond(residual)
            rho = rho_new
    return solution, residual
```

```python
import functools

import jax
import jax.numpy as jnp
from jax import lax
from jax.experimental import pallas as pl
from jax.experimental.pallas import tpu as pltpu
from jax.sharding import PartitionSpec as P

ITERS = 6
OMEGA = 0.3
DELTA = 0.9

SHIFT, DAMP, DON0, DON1 = 5, 6, 7, 13
MASK = (14, 15, 21, 22)
FLOW = 16
PA, PB = 23, 24
FEATS = 24
HALO = 16
LANES = 128
RING = 384

L2, L1, OWN, R1, R2 = 0, 8, 20, 32, 44
SLOTS = 48
RANGES = (
    ((2, 1), (8, 4), (20, 4), (32, 4), (44, 1)),
    ((8, 4), (20, 4), (32, 4)),
    ((10, 3), (20, 4), (32, 3)),
    ((12, 2), (20, 4), (32, 2)),
    ((14, 1), (20, 4), (32, 1)),
    ((20, 4),),
)
LISTS = ((L2 + 3, DON1), (L1, DON0), (L1, DON1), (OWN, DON0), (OWN, DON1), (R1, DON0), (R1, DON1), (R2, DON0))
FILLS = (
    (4, 8, 0), (6, 2, 1), (16, 20, 2), (18, 14, 3),
    (28, 32, 4), (30, 26, 5), (40, 44, 6), (42, 38, 7),
)
FILLS_AT = (range(8), (1, 2, 3, 4, 5, 6), (2, 3, 4, 5), (2, 3, 4, 5), (2, 3, 4, 5), (3, 4))


def chebyshev():
    sigma = 1.0 / DELTA
    rho = DELTA
    steps = []
    for _ in range(ITERS - 1):
        rho_new = 1.0 / (2.0 * sigma - rho)
        steps.append((rho_new * rho, 2.0 * rho_new / DELTA))
        rho = rho_new
    return steps


def pack_kernel(rhs, flow, mask, shift, damp, donors, main, strip):
    nrm = lax.axis_index("nrm")
    width = rhs.shape[2]
    here = lax.broadcasted_iota(jnp.int32, (1, width), 1) + nrm * width
    offsets = (donors[0] - here).astype(jnp.float32)
    lane = lax.broadcasted_iota(jnp.int32, (FEATS, LANES), 1)
    sent = jnp.zeros((FEATS, LANES), jnp.float32)
    for i in range(rhs.shape[1]):
        at = slice(i * width, (i + 1) * width)
        main[0:5, at] = rhs[0:5, i, :]
        main[SHIFT : SHIFT + 1, at] = shift[i : i + 1, :]
        main[DAMP : DAMP + 1, at] = damp[i : i + 1, :]
        main[DON0 : DON0 + 1, at] = offsets[0:1]
        main[8:13, at] = rhs[5:10, i, :]
        main[DON1 : DON1 + 1, at] = offsets[1:2]
        main[14:16, at] = mask[0:2, i, :].astype(jnp.float32)
        main[16:21, at] = flow[:, i, :]
        main[21:23, at] = mask[2:4, i, :].astype(jnp.float32)
        main[23:24, at] = jnp.zeros((1, width), jnp.float32)
        first = main[:, i * width : i * width + LANES]
        last = main[:, (i + 1) * width - LANES : (i + 1) * width]
        low = first if i == 0 else pltpu.roll(first, HALO * i, 1)
        turn = (HALO * (i + 1)) % LANES
        high = pltpu.roll(last, turn, 1) if turn else last
        edge = jnp.where(nrm == 0, high, low)
        sent = jnp.where((lane >= HALO * i) & (lane < HALO * (i + 1)), edge, sent)
    strip[...] = sent


def solve_kernel(left2, left1, own, right1, right2, jac, sol_out, res_out, feat, dirs, res, sol, index, basis):
    nrm = lax.axis_index("nrm")
    lane8 = lax.broadcasted_iota(jnp.int32, (8, LANES), 1)
    row8 = lax.broadcasted_iota(jnp.int32, (8, RING), 0)
    lane = lax.broadcasted_iota(jnp.int32, (FEATS, LANES), 1)
    in_halo = jnp.where(nrm == 0, lane, LANES - 1 - lane) < HALO

    j = jac[...]
    high = j.astype(jnp.bfloat16)
    low = (j - high.astype(jnp.float32)).astype(jnp.bfloat16)
    basis[:, 0:64] = high
    basis[:, 64:128] = high
    basis[:, 128:192] = low

    def precond(pa, pb, a, b):
        return pa * a + pb * b, pa * b - pb * a

    def unpack(ref, columns, first_column, slot):
        for c in range(columns):
            s = slot + c
            halo = ref[:, columns * 256 : columns * 256 + LANES]
            halo = pltpu.roll(halo, lax.rem(112 * nrm + 2 * LANES - HALO * (first_column + c), LANES), 1)
            feat[s, 0:FEATS, 0:256] = ref[:, c * 256 : (c + 1) * 256]
            feat[s, 0:FEATS, 256:RING] = jnp.where(in_halo, halo, 0.0)
            shift = feat[s, SHIFT : SHIFT + 1, :]
            scale = 1.0 / (shift * shift + OMEGA * OMEGA)
            feat[s, PA : PA + 1, :] = shift * scale
            feat[s, PB : PB + 1, :] = OMEGA * scale
            a = jnp.where(row8 < 5, feat[s, 0:8, :], 0.0)
            b = jnp.where(row8 < 5, feat[s, 8:16, :], 0.0)
            res[s, 0] = a
            res[s, 1] = b
            da, db = precond(shift * scale, OMEGA * scale, a, b)
            dirs[0, s, 0] = da
            dirs[0, s, 1] = db

    unpack(left2, 4, 4, L2)
    unpack(left1, 8, 0, L1)
    unpack(own, 8, 0, OWN)
    unpack(right1, 8, 0, R1)
    unpack(right2, 4, 0, R2)

    for n, (slot, row) in enumerate(LISTS):
        for t in range(3):
            offset = feat[slot, row : row + 1, t * LANES : (t + 1) * LANES].astype(jnp.int32)
            index[n, t] = jnp.bitwise_and(lane8 + offset, LANES - 1)

    def ghosts(par, n):
        dst, src, which = FILLS[n]
        for t in range(3):
            at = index[which, t]
            across = jnp.abs(at - lane8) > LANES // 2
            for c in range(2):
                for h in range(2):
                    tiles = [dirs[par, src + c, h, :, u * LANES : (u + 1) * LANES] for u in ((t + 2) % 3, t, (t + 1) % 3)]
                    beside = jnp.where(lane8 < LANES // 2, tiles[2], tiles[0])
                    picked = jnp.where(
                        across,
                        jnp.take_along_axis(beside, at, axis=1),
                        jnp.take_along_axis(tiles[1], at, axis=1),
                    )
                    dirs[par, dst + c, h, :, t * LANES : (t + 1) * LANES] = picked

    steps = chebyshev()

    def column(s, par, step, mine):
        d = [dirs[par, s, h] for h in range(2)]
        near = []
        for h in range(2):
            near.append(
                [
                    dirs[par, s - 1, h],
                    dirs[par, s + 1, h],
                    pltpu.roll(d[h], 1, 1),
                    pltpu.roll(d[h], RING - 1, 1),
                ]
            )
        rows = []
        for face in range(4):
            m = feat[s, MASK[face] : MASK[face] + 1, :]
            for h in range(2):
                rows.append(m * near[h][face])
        full = jnp.concatenate(rows, 0)
        high = full.astype(jnp.bfloat16)
        low = (full - high.astype(jnp.float32)).astype(jnp.bfloat16)
        return d, jnp.concatenate([high, low, high], 0)

    def finish(s, par, step, mine, d, y):
        shift = feat[s, SHIFT : SHIFT + 1, :]
        damp = feat[s, DAMP : DAMP + 1, :]
        out = [shift * d[0] - OMEGA * d[1], shift * d[1] + OMEGA * d[0]]
        for h in range(2):
            out[h] = out[h] + damp * (dirs[par, s - 2, h] + dirs[par, s + 2, h])
        for m in range(5):
            f = feat[s, FLOW + m : FLOW + m + 1, :]
            for h in range(2):
                out[h] = out[h] + f * y[16 * m + 8 * h : 16 * m + 8 * h + 8]
        new = [res[s, h] - out[h] for h in range(2)]
        for h in range(2):
            res[s, h] = new[h]
            if mine:
                sol[s - OWN, h] = d[h] if step == 0 else sol[s - OWN, h] + d[h]
        if step + 1 < ITERS:
            keep, gain = steps[step]
            pa = feat[s, PA : PA + 1, :]
            pb = feat[s, PB : PB + 1, :]
            turned = precond(pa, pb, new[0], new[1])
            for h in range(2):
                dirs[1 - par, s, h] = keep * d[h] + gain * turned[h]

    for step in range(ITERS):
        par = step % 2
        for n in FILLS_AT[step]:
            ghosts(par, n)
        for start, pairs in RANGES[step]:
            mine = start == OWN

            def body(p, carry, start=start, mine=mine, step=step, par=par):
                s = start + 2 * p
                d0, w0 = column(s, par, step, mine)
                d1, w1 = column(s + 1, par, step, mine)
                y = jnp.dot(basis[...], jnp.concatenate([w0, w1], 1), preferred_element_type=jnp.float32)
                finish(s, par, step, mine, d0, y[:, :RING])
                finish(s + 1, par, step, mine, d1, y[:, RING:])
                return carry

            lax.fori_loop(0, pairs, body, 0, unroll=True)

    for i in range(8):
        for h in range(2):
            sol_out[5 * h : 5 * h + 5, i, :] = sol[i, h, 0:5, 0:256]
            res_out[5 * h : 5 * h + 5, i, :] = res[OWN + i, h, 0:5, 0:256]


def shifted(cells, by):
    count = lax.axis_size("blk")
    return lax.ppermute(cells, "blk", [(i, i + by) for i in range(count) if 0 <= i + by < count])


def on_device(right_side, mean_flow, jac_basis, pattern, shift_diag, dissipation, donors):
    rows, width = right_side.shape[1:]
    f32 = jnp.float32
    vmem = pl.BlockSpec(memory_space=pltpu.VMEM)

    main, strip = pl.pallas_call(
        pack_kernel,
        out_shape=(
            jax.ShapeDtypeStruct((FEATS, rows * width), f32),
            jax.ShapeDtypeStruct((FEATS, LANES), f32),
        ),
        in_specs=[vmem] * 6,
        out_specs=(vmem, vmem),
    )(right_side, mean_flow, pattern, shift_diag, dissipation, donors)

    halo = lax.ppermute(strip, "nrm", [(0, 1), (1, 0)])
    half = rows * width // 2
    whole = jnp.concatenate([main, halo], 1)
    left1 = shifted(whole, 1)
    left2 = shifted(jnp.concatenate([main[:, half:], halo], 1), 2)
    right1 = shifted(whole, -1)
    right2 = shifted(jnp.concatenate([main[:, :half], halo], 1), -2)

    jac = jac_basis.reshape(4, 5, 2, 5, 2, 5).transpose(1, 2, 3, 0, 4, 5)
    jac = jnp.pad(jac, ((0, 0), (0, 0), (0, 3), (0, 0), (0, 0), (0, 3))).reshape(80, 64)

    out = jax.ShapeDtypeStruct(right_side.shape, f32)
    return pl.pallas_call(
        solve_kernel,
        out_shape=(out, out),
        in_specs=[vmem] * 6,
        out_specs=(vmem, vmem),
        scratch_shapes=[
            pltpu.VMEM((SLOTS, 32, RING), f32),
            pltpu.VMEM((2, SLOTS, 2, 8, RING), f32),
            pltpu.VMEM((SLOTS, 2, 8, RING), f32),
            pltpu.VMEM((8, 2, 8, RING), f32),
            pltpu.VMEM((8, 3, 8, LANES), jnp.int32),
            pltpu.VMEM((80, 192), jnp.bfloat16),
        ],
    )(left2, left1, whole, right1, right2, jac)


def solution(mesh):
    return jax.shard_map(
        on_device,
        mesh=mesh,
        in_specs=(
            P(None, "blk", "nrm"),
            P(None, "blk", "nrm"),
            P(),
            P(None, "blk", "nrm"),
            P("blk", "nrm"),
            P("blk", "nrm"),
            P("blk", None, "nrm"),
        ),
        out_specs=(P(None, "blk", "nrm"), P(None, "blk", "nrm")),
        check_vma=False,
    )
```

```python
import jax
import jax.numpy as jnp
from jax import lax
from jax.experimental import pallas as pl
from jax.experimental.pallas import tpu as pltpu
from jax.sharding import PartitionSpec as P


ITERS = 6
OMEGA = 0.3
DELTA = 0.9

SHIFT, DAMP, DON0, DON1 = 5, 6, 7, 13
MASK = (14, 15, 21, 22)
FLOW = 16
FEATS = 24
HALO = 16
LANES = 128
WIDTH = 256

BLOCKS = ((0, 4, 4), (8, 8, 0), (20, 8, 0), (32, 8, 0), (44, 4, 0))
FIRST = (0, 4, 12, 20, 28)
SLOTS = 48
OWN = 2
RANGES = (
    ((0, 2, 1), (1, 0, 4), (2, 0, 4), (3, 0, 4), (4, 0, 1)),
    ((1, 0, 4), (2, 0, 4), (3, 0, 4)),
    ((1, 2, 3), (2, 0, 4), (3, 0, 3)),
    ((1, 4, 2), (2, 0, 4), (3, 0, 2)),
    ((1, 6, 1), (2, 0, 4), (3, 0, 1)),
    ((2, 0, 4),),
)
STRIPS = ((0, 1, 2, 3, 4), (1, 2, 3), (1, 2, 3), (1, 2, 3), (1, 2, 3), ())
LISTS = ((0, 3, DON1), (1, 0, DON0), (1, 0, DON1), (2, 0, DON0), (2, 0, DON1), (3, 0, DON0), (3, 0, DON1), (4, 0, DON0))
FILLS = (
    (4, 8, 0), (6, 2, 1), (16, 20, 2), (18, 14, 3),
    (28, 32, 4), (30, 26, 5), (40, 44, 6), (42, 38, 7),
)
FILLS_AT = (range(8), (1, 2, 3, 4, 5, 6), (2, 3, 4, 5), (2, 3, 4, 5), (2, 3, 4, 5), (3, 4))


def chebyshev():
    sigma = 1.0 / DELTA
    rho = DELTA
    steps = []
    for _ in range(ITERS - 1):
        rho_new = 1.0 / (2.0 * sigma - rho)
        steps.append((rho_new * rho, 2.0 * rho_new / DELTA))
        rho = rho_new
    return steps


def split(full):
    high = full.astype(jnp.bfloat16)
    return high, (full - high.astype(jnp.float32)).astype(jnp.bfloat16)


def precond(pa, pb, a, b):
    return pa * a + pb * b, pa * b - pb * a


def lanes(rows):
    return lax.broadcasted_iota(jnp.int32, (rows, LANES), 1)


def pack_kernel(rhs, flow, mask, shift, damp, donors, whole, lower, upper):
    nrm = lax.axis_index("nrm")
    count, width = rhs.shape[1:]
    here = lax.broadcasted_iota(jnp.int32, (1, width), 1) + nrm * width
    offsets = (donors[0] - here).astype(jnp.float32)
    half = count * width // 2
    for i in range(count):
        side = lower if i < count // 2 else upper
        start = i * width % half
        for out, at in ((whole, slice(i * width, (i + 1) * width)), (side, slice(start, start + width))):
            out[0:5, at] = rhs[0:5, i, :]
            out[SHIFT : SHIFT + 1, at] = shift[i : i + 1, :]
            out[DAMP : DAMP + 1, at] = damp[i : i + 1, :]
            out[DON0 : DON0 + 1, at] = offsets[0:1]
            out[8:13, at] = rhs[5:10, i, :]
            out[DON1 : DON1 + 1, at] = offsets[1:2]
            out[14:16, at] = mask[0:2, i, :].astype(jnp.float32)
            out[16:21, at] = flow[:, i, :]
            out[21:23, at] = mask[2:4, i, :].astype(jnp.float32)
            out[23:24, at] = jnp.zeros((1, width), jnp.float32)


def basis_kernel(jac, basis, full):
    full[...] = jnp.zeros(full.shape, jnp.float32)
    for f in range(4):
        for m in range(5):
            for h in range(2):
                for g in range(2):
                    block = jac[m, 5 * h : 5 * h + 5, f, 5 * g : 5 * g + 5]
                    full[16 * m + 8 * h : 16 * m + 8 * h + 5, 16 * f + 8 * g : 16 * f + 8 * g + 5] = block
    high, low = split(full[...])
    basis[:, 0:64] = high
    basis[:, 64:128] = high
    basis[:, 128:192] = low


def strip_kernel(*refs):
    nrm = lax.axis_index("nrm")
    strip = refs[-1]
    lane = lanes(FEATS)
    for b, (ref, (_, held, first)) in enumerate(zip(refs[:-1], BLOCKS, strict=True)):
        sent = jnp.zeros((FEATS, LANES), jnp.float32)
        for c in range(held):
            at = pl.ds(pl.multiple_of(c * WIDTH + (1 - nrm) * LANES, LANES), LANES)
            col = first + c
            edge = pltpu.roll(ref[:, at], lax.rem(HALO * (col + 1 - nrm), LANES), 1)
            sent = jnp.where((lane >= HALO * col) & (lane < HALO * (col + 1)), edge, sent)
        strip[:, b * LANES : (b + 1) * LANES] = sent


def ghosts(src_d, dst_d, dst_h, index, n):
    dst, src, which = FILLS[n]
    lane = lanes(8)
    for c in range(2):
        for t in range(2):
            at = index[which, t]
            across = jnp.abs(at - lane) > LANES // 2
            picked = []
            for h in range(2):
                tiles = [src_d[src + c, h, :, u * LANES : (u + 1) * LANES] for u in (t, 1 - t)]
                here, there = (jnp.take_along_axis(x, at, axis=1) for x in tiles)
                picked.append(jnp.where(across, there, here))
                dst_d[dst + c, h, :, t * LANES : (t + 1) * LANES] = picked[h]
            high, low = split(jnp.concatenate(picked, 0))
            dst_h[dst + c, 0, :, t * LANES : (t + 1) * LANES] = high
            dst_h[dst + c, 1, :, t * LANES : (t + 1) * LANES] = low


def prep_kernel(left2, left1, own, right1, right2, coef, masks, res, dirs, parts, index):
    nrm = lax.axis_index("nrm")
    refs = (left2, left1, own, right1, right2)
    row = lax.broadcasted_iota(jnp.int32, (8, WIDTH), 0)
    lane = lax.broadcasted_iota(jnp.int32, (16, WIDTH), 1)
    wall = ((lane == 0) & (nrm == 0), (lane == WIDTH - 1) & (nrm == 1))
    for ref, (slot, held, _), first in zip(refs, BLOCKS, FIRST, strict=True):
        for c in range(held):
            q, s = first + c, slot + c
            at = slice(c * WIDTH, (c + 1) * WIDTH)
            shift = ref[SHIFT : SHIFT + 1, at]
            scale = 1.0 / (shift * shift + OMEGA * OMEGA)
            pa, pb = shift * scale, OMEGA * scale
            coef[q, 0:1] = shift
            coef[q, 1:2] = ref[DAMP : DAMP + 1, at]
            coef[q, 2:3] = pa
            coef[q, 3:4] = pb
            coef[q, 8:16] = ref[FLOW : FLOW + 8, at]
            for face in range(4):
                m = jnp.broadcast_to(ref[MASK[face] : MASK[face] + 1, at], (16, WIDTH))
                if face >= 2:
                    m = jnp.where(wall[face - 2], 0.0, m)
                masks[q, face] = m.astype(jnp.bfloat16)
            a = jnp.where(row < 5, ref[0:8, at], 0.0)
            b = jnp.where(row < 5, ref[8:16, at], 0.0)
            res[q, 0] = a
            res[q, 1] = b
            da, db = precond(pa, pb, a, b)
            dirs[s, 0] = da
            dirs[s, 1] = db
            high, low = split(jnp.concatenate([da, db], 0))
            parts[s, 0] = high
            parts[s, 1] = low
    for n, (b, c, r) in enumerate(LISTS):
        for t in range(2):
            start = c * WIDTH + t * LANES
            offset = refs[b][r : r + 1, start : start + LANES].astype(jnp.int32)
            index[n, t] = jnp.bitwise_and(lanes(8) + offset, LANES - 1)
    for n in FILLS_AT[0]:
        ghosts(dirs, dirs, parts, index, n)


def solve_kernel(
    coef, masks, res0, dirs0, parts0, index, halo, basis, sol_out, res_out,
    dirs, parts, res, sol, sdirs, sparts, sres, spre,
):
    nrm = lax.axis_index("nrm")
    lane = lanes(8)
    lane16 = lanes(16)
    group = jnp.bitwise_and(lane, HALO - 1)
    low_rows = lax.broadcasted_iota(jnp.int32, (8, LANES), 0) < 5
    steps = chebyshev()

    def dirs_at(step):
        return dirs0 if step == 0 else dirs.at[step % 2]

    def parts_at(step):
        return parts0 if step == 0 else parts.at[step % 2]

    def store_strip(par, b, values):
        for h in range(2):
            sdirs[par, b, h] = values[h]
        high, low = split(jnp.concatenate(values, 0))
        sparts[par, b, 0] = high
        sparts[par, b, 1] = low

    for b in range(5):
        at = slice(b * LANES, (b + 1) * LANES)
        shift = halo[SHIFT : SHIFT + 1, at]
        scale = 1.0 / (shift * shift + OMEGA * OMEGA)
        spre[b, 0:1] = shift * scale
        spre[b, 1:2] = OMEGA * scale
        x = [jnp.where(low_rows, halo[8 * h : 8 * h + 8, at], 0.0) for h in range(2)]
        for h in range(2):
            sres[b, h] = x[h]
        store_strip(0, b, list(precond(shift * scale, OMEGA * scale, *x)))

    def apply(d, far, y, shift, damp, flow):
        out = [shift * d[0] - OMEGA * d[1], shift * d[1] + OMEGA * d[0]]
        for h in range(2):
            out[h] = out[h] + damp * far[h]
        for m in range(5):
            f = flow(m)
            for h in range(2):
                out[h] = out[h] + f * y[16 * m + 8 * h : 16 * m + 8 * h + 8]
        return out

    def strips(step):
        par = step % 2
        source = dirs_at(step)
        for b in STRIPS[step]:
            slot, held, first = BLOCKS[b]
            at = slice(b * LANES, (b + 1) * LANES)
            before = halo[DON0 : DON0 + 1, at].astype(jnp.int32) + lane
            after = halo[DON1 : DON1 + 1, at].astype(jnp.int32) + lane
            rows, far, mid = [[], [], [], []], [], []
            for h in range(2):
                d = sdirs[par, b, h]
                edge = jnp.zeros((8, LANES), jnp.float32)
                for c in range(held):
                    col = first + c
                    tile = source[slot + c, h, :, pl.ds(pl.multiple_of((1 - nrm) * LANES, LANES), LANES)]
                    tile = pltpu.roll(tile, HALO * col + 1 + 14 * nrm, 1)
                    edge = jnp.where((lane >= HALO * col) & (lane < HALO * (col + 1)), tile, edge)
                west, west2 = pltpu.roll(d, HALO, 1), pltpu.roll(d, 2 * HALO, 1)
                east, east2 = pltpu.roll(d, LANES - HALO, 1), pltpu.roll(d, LANES - 2 * HALO, 1)
                if b > 0:
                    other = sdirs[par, b - 1, h]
                    near = jnp.take_along_axis(other, jnp.bitwise_and(before + 7 * HALO, LANES - 1), axis=1)
                    next2 = jnp.take_along_axis(other, jnp.bitwise_and(before + 6 * HALO, LANES - 1), axis=1)
                    west = jnp.where(lane < HALO, near, west)
                    west2 = jnp.where(lane < 2 * HALO, next2, west2)
                if b < 4:
                    other = sdirs[par, b + 1, h]
                    near = jnp.take_along_axis(other, jnp.bitwise_and(after + HALO, LANES - 1), axis=1)
                    next2 = jnp.take_along_axis(other, jnp.bitwise_and(after + 2 * HALO, LANES - 1), axis=1)
                    east = jnp.where(lane >= 7 * HALO, near, east)
                    east2 = jnp.where(lane >= 6 * HALO, next2, east2)
                south = jnp.where(group == 0, edge, pltpu.roll(d, 1, 1))
                north = jnp.where(group == HALO - 1, edge, pltpu.roll(d, LANES - 1, 1))
                for face, value in enumerate((west, east, south, north)):
                    rows[face].append(halo[MASK[face] : MASK[face] + 1, at] * value)
                far.append(west2 + east2)
                mid.append(d)
            high, low = split(jnp.concatenate(sum(rows, []), 0))
            y = jnp.dot(basis[...], jnp.concatenate([high, low, high], 0), preferred_element_type=jnp.float32)
            out = apply(
                mid, far, y, halo[SHIFT : SHIFT + 1, at], halo[DAMP : DAMP + 1, at],
                lambda m, at=at: halo[FLOW + m : FLOW + m + 1, at],
            )
            new = [sres[b, h] - out[h] for h in range(2)]
            for h in range(2):
                sres[b, h] = new[h]
            keep, gain = steps[step]
            turned = precond(spre[b, 0:1], spre[b, 1:2], *new)
            store_strip(1 - par, b, [keep * mid[h] + gain * turned[h] for h in range(2)])

    def column(step, b, c):
        slot, _, first = BLOCKS[b]
        s, q = slot + c, FIRST[b] + c
        par = step % 2
        p = parts_at(step)
        turn = 127 - 14 * nrm - HALO * (first + c)
        stack = [[], []]
        for k in range(2):
            tiles = [p[s, k, :, t * LANES : (t + 1) * LANES] for t in range(2)]
            edge = pltpu.roll(sparts[par, b, k], turn, 1)
            up = [pltpu.roll(x, 1, 1) for x in tiles]
            down = [pltpu.roll(x, LANES - 1, 1) for x in tiles]
            south = [jnp.where(lane16 == 0, edge, up[0]), jnp.where(lane16 == 0, up[0], up[1])]
            north = [jnp.where(lane16 == LANES - 1, down[1], down[0]), jnp.where(lane16 == LANES - 1, edge, down[1])]
            for face, value in enumerate(
                (p[s - 1, k], p[s + 1, k], jnp.concatenate(south, 1), jnp.concatenate(north, 1))
            ):
                stack[k].append(masks[q, face] * value)
        return jnp.concatenate(stack[0] + stack[1] + stack[0], 0)

    def finish(step, b, c, y):
        s, q = BLOCKS[b][0] + c, FIRST[b] + c
        d = dirs_at(step)
        mid = [d[s, h] for h in range(2)]
        far = [d[s - 2, h] + d[s + 2, h] for h in range(2)]
        out = apply(mid, far, y, coef[q, 0:1], coef[q, 1:2], lambda m: coef[q, 8 + m : 9 + m])
        old = res0 if step == 0 else res
        new = [old[q, h] - out[h] for h in range(2)]
        for h in range(2):
            res[q, h] = new[h]
            if b == OWN:
                sol[c, h] = mid[h] if step == 0 else sol[c, h] + mid[h]
        if step + 1 < ITERS:
            keep, gain = steps[step]
            turned = precond(coef[q, 2:3], coef[q, 3:4], *new)
            made = [keep * mid[h] + gain * turned[h] for h in range(2)]
            par = 1 - step % 2
            for h in range(2):
                dirs[par, s, h] = made[h]
            high, low = split(jnp.concatenate(made, 0))
            parts[par, s, 0] = high
            parts[par, s, 1] = low

    for step in range(ITERS):
        if step:
            par = step % 2
            for n in FILLS_AT[step]:
                ghosts(dirs.at[par], dirs.at[par], parts.at[par], index, n)
        strips(step)
        for b, start, pairs in RANGES[step]:

            def body(p, carry, step=step, b=b, start=start):
                for k in range(2):
                    c = start + 2 * p + k
                    y = jnp.dot(basis[...], column(step, b, c), preferred_element_type=jnp.float32)
                    finish(step, b, c, y)
                return carry

            lax.fori_loop(0, pairs, body, 0, unroll=UNROLL)

    for i in range(8):
        for h in range(2):
            sol_out[5 * h : 5 * h + 5, i, :] = sol[i, h, 0:5]
            res_out[5 * h : 5 * h + 5, i, :] = res[FIRST[OWN] + i, h, 0:5]


UNROLL = True


def shifted(cells, by):
    count = lax.axis_size("blk")
    return lax.ppermute(cells, "blk", [(i, i + by) for i in range(count) if 0 <= i + by < count])


def local(kernel, outs, scratch, *args, limit=16 << 20):
    vmem = pl.BlockSpec(memory_space=pltpu.VMEM)
    return pl.pallas_call(
        kernel,
        out_shape=outs,
        in_specs=[vmem] * len(args),
        out_specs=jax.tree.map(lambda _: vmem, outs),
        scratch_shapes=scratch,
        compiler_params=pltpu.CompilerParams(vmem_limit_bytes=limit),
    )(*args)


def inside(x):
    return pltpu.with_memory_space_constraint(x, pltpu.VMEM)


def step(right_side, mean_flow, jac_basis, pattern, shift_diag, dissipation, donors):
    rows, width = right_side.shape[1:]
    f32, bf16 = jnp.float32, jnp.bfloat16
    vmem = pltpu.VMEM
    half = rows * width // 2

    whole, lower, upper = local(
        pack_kernel,
        (vmem((FEATS, 2 * half), f32), vmem((FEATS, half), f32), vmem((FEATS, half), f32)),
        [],
        right_side, mean_flow, pattern, shift_diag, dissipation, donors,
        limit=None,
    )
    left1 = shifted(whole, 1)
    left2 = shifted(upper, 2)
    right1 = shifted(whole, -1)
    right2 = shifted(lower, -2)
    basis = local(
        basis_kernel, vmem((80, 192), bf16), [vmem((80, 64), f32)], jac_basis.transpose(1, 2, 0, 3)
    )

    cells = [inside(x) for x in (left2, left1, whole, right1, right2)]
    strip = local(strip_kernel, vmem((FEATS, 5 * LANES), f32), [], *cells)
    halo = lax.ppermute(strip, "nrm", [(0, 1), (1, 0)])
    ready = local(
        prep_kernel,
        (
            vmem((32, 16, WIDTH), f32),
            vmem((32, 4, 16, WIDTH), bf16),
            vmem((32, 2, 8, WIDTH), f32),
            vmem((SLOTS, 2, 8, WIDTH), f32),
            vmem((SLOTS, 2, 16, WIDTH), bf16),
            vmem((8, 2, 8, LANES), jnp.int32),
        ),
        [],
        *cells,
    )

    out = jax.ShapeDtypeStruct(right_side.shape, f32)
    scratch = [
        vmem((2, SLOTS, 2, 8, WIDTH), f32),
        vmem((2, SLOTS, 2, 16, WIDTH), bf16),
        vmem((32, 2, 8, WIDTH), f32),
        vmem((8, 2, 8, WIDTH), f32),
        vmem((2, 5, 2, 8, LANES), f32),
        vmem((2, 5, 2, 16, LANES), bf16),
        vmem((5, 2, 8, LANES), f32),
        vmem((5, 8, LANES), f32),
    ]
    return local(
        solve_kernel, (out, out), scratch, *[inside(x) for x in ready], inside(halo), inside(basis)
    )


def solution(mesh):
    return jax.shard_map(
        step,
        mesh=mesh,
        in_specs=(
            P(None, "blk", "nrm"),
            P(None, "blk", "nrm"),
            P(),
            P(None, "blk", "nrm"),
            P("blk", "nrm"),
            P("blk", "nrm"),
            P("blk", None, "nrm"),
        ),
        out_specs=(P(None, "blk", "nrm"), P(None, "blk", "nrm")),
        check_vma=False,
    )
```

```python
import functools

import jax
import jax.numpy as jnp
from jax import lax
from jax.experimental import pallas as pl
from jax.experimental.pallas import tpu as pltpu
from jax.sharding import PartitionSpec as P


ITERS = 6
OMEGA = 0.3
DELTA = 0.9

SHIFT, DAMP, DON0, DON1 = 5, 6, 7, 13
MASK = (14, 15, 21, 22)
FLOW = 16
FEATS = 24
HALO = 16
LANES = 128
WIDTH = 256

FAR1, OWN, NEAR = 1, 2, 3
BLOCKS = ((0, 4, 4, 4), (8, 8, 0, 8), (20, 8, 0, 8), (32, 6, 0, 8))
FIRST = (0, 4, 12, 20)
COLUMNS = 26
SLOTS = 38
MIDDLE = 3
RANGES = (
    ((0, 2, 1), (1, 0, 4), (2, 0, 4), (3, 0, 2)),
    ((1, 0, 4), (2, 0, 4), (3, 0, 1)),
    ((1, 2, 3), (2, 0, 4)),
    ((1, 4, 2), (2, 0, 4), (3, 0, 2)),
    ((1, 6, 1), (2, 0, 4), (3, 0, 1)),
    ((2, 0, 4),),
)
STRIPS = ((0, 1, 2, 3), (1, 2, 3), (1, 2), (1, 2, 3), (2,), ())
LISTS = ((0, 3, 1), (1, 0, 0), (1, 0, 1), (2, 0, 0), (2, 0, 1), (3, 0, 0))
FILLS = ((4, 8, 0), (6, 2, 1), (16, 20, 2), (18, 14, 3), (28, 32, 4), (30, 26, 5))
FILLS_AT = ((0, 1, 2, 3, 4, 5), (1, 2, 3, 4, 5), (2, 3, 4), (2, 3, 4, 5), (2, 3, 4, 5), (3, 4))
SENT_DIRS, SENT_RES = 6, 4


def chebyshev():
    sigma = 1.0 / DELTA
    rho = DELTA
    steps = []
    for _ in range(ITERS - 1):
        rho_new = 1.0 / (2.0 * sigma - rho)
        steps.append((rho_new * rho, 2.0 * rho_new / DELTA))
        rho = rho_new
    return steps


def split(full):
    high = full.astype(jnp.bfloat16)
    return high, (full - high.astype(jnp.float32)).astype(jnp.bfloat16)


def precond(pa, pb, a, b):
    return pa * a + pb * b, pa * b - pb * a


def lanes(rows):
    return lax.broadcasted_iota(jnp.int32, (rows, LANES), 1)


def mirrored():
    return lax.rem(lax.axis_index("blk"), 2)


def place(b, c, odd):
    _, _, _, sent = BLOCKS[b]
    return c + odd * (sent - 1 - 2 * c)


def pack_kernel(rhs, flow, mask, shift, damp, donors, whole, part):
    nrm = lax.axis_index("nrm")
    count, width = rhs.shape[1:]
    here = lax.broadcasted_iota(jnp.int32, (1, width), 1) + nrm * width
    offsets = (donors[0] - here).astype(jnp.float32)
    for i in range(count):
        at = slice(i * width, (i + 1) * width)
        whole[0:5, at] = rhs[0:5, i, :]
        whole[SHIFT : SHIFT + 1, at] = shift[i : i + 1, :]
        whole[DAMP : DAMP + 1, at] = damp[i : i + 1, :]
        whole[DON0 : DON0 + 1, at] = offsets[0:1]
        whole[8:13, at] = rhs[5:10, i, :]
        whole[DON1 : DON1 + 1, at] = offsets[1:2]
        whole[14:16, at] = mask[0:2, i, :].astype(jnp.float32)
        whole[16:21, at] = flow[:, i, :]
        whole[21:23, at] = mask[2:4, i, :].astype(jnp.float32)
        whole[23:24, at] = jnp.zeros((1, width), jnp.float32)
    half = count * width // 2
    part[...] = whole[:, pl.ds(pl.multiple_of((1 - mirrored()) * half, LANES), half)]


def basis_kernel(jac, basis, full):
    full[...] = jnp.zeros(full.shape, jnp.float32)
    for f in range(4):
        for m in range(5):
            for h in range(2):
                for g in range(2):
                    block = jac[m, 5 * h : 5 * h + 5, f, 5 * g : 5 * g + 5]
                    full[16 * m + 8 * h : 16 * m + 8 * h + 5, 16 * f + 8 * g : 16 * f + 8 * g + 5] = block
    j = full[...]
    lane = lanes(80)
    other = jnp.where(lane < 16, pltpu.roll(j, LANES - 16, 1), pltpu.roll(j, 16, 1))
    j = jnp.where((mirrored() == 1) & (lane < 32), other, j)[:, 0:64]
    high, low = split(j)
    basis[:, 0:64] = high
    basis[:, 64:128] = high
    basis[:, 128:192] = low


def strip_kernel(*refs):
    nrm, odd = lax.axis_index("nrm"), mirrored()
    strip = refs[-1]
    lane = lanes(FEATS)
    for b, ref in enumerate(refs[:-1]):
        first, sent = BLOCKS[b][2:]
        rows = jnp.zeros((FEATS, LANES), jnp.float32)
        for c in range(sent):
            start = place(b, c, odd) * WIDTH + (1 - nrm) * LANES
            col = first + c
            edge = ref[:, pl.ds(pl.multiple_of(start, LANES), LANES)]
            edge = pltpu.roll(edge, lax.rem(HALO * (col + 1 - nrm), LANES), 1)
            rows = jnp.where((lane >= HALO * col) & (lane < HALO * (col + 1)), edge, rows)
        strip[:, b * LANES : (b + 1) * LANES] = rows


def ghosts(src_d, dst_d, dst_h, index, n):
    dst, src, which = FILLS[n]
    lane = lanes(8)
    for c in range(2):
        for t in range(2):
            at = index[which, t]
            across = jnp.abs(at - lane) > LANES // 2
            picked = []
            for h in range(2):
                tiles = [src_d[src + c, h, :, u * LANES : (u + 1) * LANES] for u in (t, 1 - t)]
                here, there = (jnp.take_along_axis(x, at, axis=1) for x in tiles)
                picked.append(jnp.where(across, there, here))
                dst_d[dst + c, h, :, t * LANES : (t + 1) * LANES] = picked[h]
            high, low = split(jnp.concatenate(picked, 0))
            dst_h[dst + c, 0, :, t * LANES : (t + 1) * LANES] = high
            dst_h[dst + c, 1, :, t * LANES : (t + 1) * LANES] = low


def prep_kernel(far2, far1, own, near, coef, masks, res, dirs, parts, index):
    nrm, odd = lax.axis_index("nrm"), mirrored()
    refs = (far2, far1, own, near)
    row = lax.broadcasted_iota(jnp.int32, (8, WIDTH), 0)
    lane = lax.broadcasted_iota(jnp.int32, (16, WIDTH), 1)
    wall = ((lane == 0) & (nrm == 0), (lane == WIDTH - 1) & (nrm == 1))
    for b, ref in enumerate(refs):
        slot, held = BLOCKS[b][:2]
        for c in range(held):
            q, s = FIRST[b] + c, slot + c
            at = pl.ds(pl.multiple_of(place(b, c, odd) * WIDTH, WIDTH), WIDTH)
            shift = ref[SHIFT : SHIFT + 1, at]
            scale = 1.0 / (shift * shift + OMEGA * OMEGA)
            pa, pb = shift * scale, OMEGA * scale
            coef[q, 0:1] = shift
            coef[q, 1:2] = ref[DAMP : DAMP + 1, at]
            coef[q, 2:3] = pa
            coef[q, 3:4] = pb
            coef[q, 8:16] = ref[FLOW : FLOW + 8, at]
            m = [ref[MASK[face] : MASK[face] + 1, at] for face in range(4)]
            m[0], m[1] = jnp.where(odd == 1, m[1], m[0]), jnp.where(odd == 1, m[0], m[1])
            for face in range(4):
                wide = jnp.broadcast_to(m[face], (16, WIDTH))
                if face >= 2:
                    wide = jnp.where(wall[face - 2], 0.0, wide)
                masks[q, face] = wide.astype(jnp.bfloat16)
            x = jnp.where(row < 5, ref[0:8, at], 0.0)
            y = jnp.where(row < 5, ref[8:16, at], 0.0)
            res[q, 0] = x
            res[q, 1] = y
            dx, dy = precond(pa, pb, x, y)
            dirs[s, 0] = dx
            dirs[s, 1] = dy
            high, low = split(jnp.concatenate([dx, dy], 0))
            parts[s, 0] = high
            parts[s, 1] = low
    for n, (b, c, side) in enumerate(LISTS):
        for t in range(2):
            at = slice(c * WIDTH + t * LANES, c * WIDTH + (t + 1) * LANES)
            pair = [refs[b][r : r + 1, at] for r in (DON0, DON1)]
            offset = jnp.where(odd == 1, pair[1 - side], pair[side]).astype(jnp.int32)
            index[n, t] = jnp.bitwise_and(lanes(8) + offset, LANES - 1)
    for n in FILLS_AT[0]:
        ghosts(dirs, dirs, parts, index, n)


def near_message(message, dirs, res, sdirs, sres):
    for n in range(SENT_DIRS):
        for h in range(2):
            message[8 * (2 * n + h) : 8 * (2 * n + h) + 8, :] = dirs[BLOCKS[OWN][0] + 7 - n, h]
    for n in range(SENT_RES):
        for h in range(2):
            at = 16 * SENT_DIRS + 8 * (2 * n + h)
            message[at : at + 8, :] = res[FIRST[OWN] + 7 - n, h]
    at = 16 * (SENT_DIRS + SENT_RES)
    for h in range(2):
        message[at + 8 * h : at + 8 * h + 8, 0:LANES] = sdirs[OWN, h]
        message[at + 8 * h : at + 8 * h + 8, LANES:] = sres[OWN, h]


def solve_kernel(begin, *refs):
    if begin == 0:
        (coef, masks, res0, dirs0, parts0, index, halo, basis) = refs[:8]
        (dirs, res, sol, sdirs, sres, message, parts, sparts, spre, sdon) = refs[8:]
        end = MIDDLE
    else:
        (coef, masks, old_dirs, old_res, old_sol, old_sdirs, old_sres, message, index, halo, basis) = refs[:11]
        (sol_out, res_out, dirs, res, sol, sdirs, sres, parts, sparts, spre, sdon) = refs[11:]
        end = ITERS
    nrm, odd = lax.axis_index("nrm"), mirrored()
    lane = lanes(8)
    lane16 = lanes(16)
    group = jnp.bitwise_and(lane, HALO - 1)
    low_rows = lax.broadcasted_iota(jnp.int32, (8, LANES), 0) < 5
    steps = chebyshev()

    def dirs_at(step):
        return dirs0 if step == 0 else dirs.at[step % 2]

    def parts_at(step):
        return parts0 if step == 0 else parts.at[step % 2]

    def store(par, s, values):
        for h in range(2):
            dirs[par, s, h] = values[h]
        high, low = split(jnp.concatenate(values, 0))
        parts[par, s, 0] = high
        parts[par, s, 1] = low

    def store_strip(par, b, values):
        for h in range(2):
            sdirs[par, b, h] = values[h]
        high, low = split(jnp.concatenate(values, 0))
        sparts[par, b, 0] = high
        sparts[par, b, 1] = low

    for b in range(4):
        at = slice(b * LANES, (b + 1) * LANES)
        shift = halo[SHIFT : SHIFT + 1, at]
        scale = 1.0 / (shift * shift + OMEGA * OMEGA)
        spre[b, 0:1] = shift * scale
        spre[b, 1:2] = OMEGA * scale
        m = [halo[MASK[face] : MASK[face] + 1, at] for face in range(4)]
        spre[b, 2:3] = jnp.where(odd == 1, m[1], m[0])
        spre[b, 3:4] = jnp.where(odd == 1, m[0], m[1])
        spre[b, 4:5] = m[2]
        spre[b, 5:6] = m[3]
        pair = [halo[r : r + 1, at] for r in (DON0, DON1)]
        sdon[b, 0] = jnp.where(odd == 1, pair[1], pair[0]).astype(jnp.int32) + lane
        sdon[b, 1] = jnp.where(odd == 1, pair[0], pair[1]).astype(jnp.int32) + lane
        if begin == 0:
            x = [jnp.where(low_rows, halo[8 * h : 8 * h + 8, at], 0.0) for h in range(2)]
            for h in range(2):
                sres[b, h] = x[h]
            store_strip(0, b, list(precond(shift * scale, OMEGA * scale, *x)))

    if begin:
        par = begin % 2
        for b, kept in ((FAR1, range(2, 8)), (OWN, range(8))):
            for c in kept:
                s, q = BLOCKS[b][0] + c, FIRST[b] + c
                store(par, s, [old_dirs[par, s, h] for h in range(2)])
                for h in range(2):
                    res[q, h] = old_res[q, h]
            store_strip(par, b, [old_sdirs[par, b, h] for h in range(2)])
            for h in range(2):
                sres[b, h] = old_sres[b, h]
        for c in range(8):
            for h in range(2):
                sol[c, h] = old_sol[c, h]
        slot, first = BLOCKS[NEAR][0], FIRST[NEAR]
        for n in range(SENT_DIRS):
            at = 16 * n
            store(par, slot + n, [message[at + 8 * h : at + 8 * h + 8, :] for h in range(2)])
        for n in range(SENT_RES):
            for h in range(2):
                at = 16 * (SENT_DIRS + n) + 8 * h
                res[first + n, h] = message[at : at + 8, :]
        swap = 7 * HALO - (lane - group) + group
        at = 16 * (SENT_DIRS + SENT_RES)
        values = []
        for h in range(2):
            rows = slice(at + 8 * h, at + 8 * h + 8)
            values.append(jnp.take_along_axis(message[rows, 0:LANES], swap, axis=1))
            sres[NEAR, h] = jnp.take_along_axis(message[rows, LANES:], swap, axis=1)
        store_strip(par, NEAR, values)

    def apply(d, far, y, shift, damp, flow):
        out = [shift * d[0] - OMEGA * d[1], shift * d[1] + OMEGA * d[0]]
        for h in range(2):
            out[h] = out[h] + damp * far[h]
        for m in range(5):
            f = flow(m)
            for h in range(2):
                out[h] = out[h] + f * y[16 * m + 8 * h : 16 * m + 8 * h + 8]
        return out

    def strips(step):
        par = step % 2
        source = dirs_at(step)
        for b in STRIPS[step]:
            slot, held, first, _ = BLOCKS[b]
            at = slice(b * LANES, (b + 1) * LANES)
            before, after = sdon[b, 0], sdon[b, 1]
            rows, far, mid = [[], [], [], []], [], []
            for h in range(2):
                d = sdirs[par, b, h]
                edge = jnp.zeros((8, LANES), jnp.float32)
                for c in range(held):
                    col = first + c
                    tile = source[slot + c, h, :, pl.ds(pl.multiple_of((1 - nrm) * LANES, LANES), LANES)]
                    tile = pltpu.roll(tile, HALO * col + 1 + 14 * nrm, 1)
                    edge = jnp.where((lane >= HALO * col) & (lane < HALO * (col + 1)), tile, edge)
                west, west2 = pltpu.roll(d, HALO, 1), pltpu.roll(d, 2 * HALO, 1)
                east, east2 = pltpu.roll(d, LANES - HALO, 1), pltpu.roll(d, LANES - 2 * HALO, 1)
                if b > 0:
                    other = sdirs[par, b - 1, h]
                    close = jnp.take_along_axis(other, jnp.bitwise_and(before + 7 * HALO, LANES - 1), axis=1)
                    next2 = jnp.take_along_axis(other, jnp.bitwise_and(before + 6 * HALO, LANES - 1), axis=1)
                    west = jnp.where(lane < HALO, close, west)
                    west2 = jnp.where(lane < 2 * HALO, next2, west2)
                if b < 3:
                    other = sdirs[par, b + 1, h]
                    close = jnp.take_along_axis(other, jnp.bitwise_and(after + HALO, LANES - 1), axis=1)
                    next2 = jnp.take_along_axis(other, jnp.bitwise_and(after + 2 * HALO, LANES - 1), axis=1)
                    east = jnp.where(lane >= 7 * HALO, close, east)
                    east2 = jnp.where(lane >= 6 * HALO, next2, east2)
                south = jnp.where(group == 0, edge, pltpu.roll(d, 1, 1))
                north = jnp.where(group == HALO - 1, edge, pltpu.roll(d, LANES - 1, 1))
                for face, value in enumerate((west, east, south, north)):
                    rows[face].append(spre[b, 2 + face : 3 + face] * value)
                far.append(west2 + east2)
                mid.append(d)
            high, low = split(jnp.concatenate(sum(rows, []), 0))
            y = jnp.dot(basis[...], jnp.concatenate([high, low, high], 0), preferred_element_type=jnp.float32)
            out = apply(
                mid, far, y, halo[SHIFT : SHIFT + 1, at], halo[DAMP : DAMP + 1, at],
                lambda m, at=at: halo[FLOW + m : FLOW + m + 1, at],
            )
            new = [sres[b, h] - out[h] for h in range(2)]
            for h in range(2):
                sres[b, h] = new[h]
            keep, gain = steps[step]
            turned = precond(spre[b, 0:1], spre[b, 1:2], *new)
            store_strip(1 - par, b, [keep * mid[h] + gain * turned[h] for h in range(2)])

    def column(step, b, c):
        slot, _, first, _ = BLOCKS[b]
        s, q = slot + c, FIRST[b] + c
        par = step % 2
        p = parts_at(step)
        turn = 127 - 14 * nrm - HALO * (first + c)
        stack = [[], []]
        for k in range(2):
            tiles = [p[s, k, :, t * LANES : (t + 1) * LANES] for t in range(2)]
            edge = pltpu.roll(sparts[par, b, k], turn, 1)
            up = [pltpu.roll(x, 1, 1) for x in tiles]
            down = [pltpu.roll(x, LANES - 1, 1) for x in tiles]
            south = [jnp.where(lane16 == 0, edge, up[0]), jnp.where(lane16 == 0, up[0], up[1])]
            north = [jnp.where(lane16 == LANES - 1, down[1], down[0]), jnp.where(lane16 == LANES - 1, edge, down[1])]
            for face, value in enumerate(
                (p[s - 1, k], p[s + 1, k], jnp.concatenate(south, 1), jnp.concatenate(north, 1))
            ):
                stack[k].append(masks[q, face] * value)
        return jnp.concatenate(stack[0] + stack[1] + stack[0], 0)

    def finish(step, b, c, y):
        s, q = BLOCKS[b][0] + c, FIRST[b] + c
        d = dirs_at(step)
        mid = [d[s, h] for h in range(2)]
        far = [d[s - 2, h] + d[s + 2, h] for h in range(2)]
        out = apply(mid, far, y, coef[q, 0:1], coef[q, 1:2], lambda m: coef[q, 8 + m : 9 + m])
        old = res0 if step == 0 else res
        new = [old[q, h] - out[h] for h in range(2)]
        for h in range(2):
            res[q, h] = new[h]
            if b == OWN:
                sol[c, h] = mid[h] if step == 0 else sol[c, h] + mid[h]
        if step + 1 < ITERS:
            keep, gain = steps[step]
            turned = precond(coef[q, 2:3], coef[q, 3:4], *new)
            store(1 - step % 2, s, [keep * mid[h] + gain * turned[h] for h in range(2)])

    for step in range(begin, end):
        if step:
            par = step % 2
            for n in FILLS_AT[step]:
                ghosts(dirs.at[par], dirs.at[par], parts.at[par], index, n)
        strips(step)
        for b, start, pairs in RANGES[step]:
            for c in range(start, start + 2 * pairs):
                y = jnp.dot(basis[...], column(step, b, c), preferred_element_type=jnp.float32)
                finish(step, b, c, y)

    if begin == 0:
        par = end % 2
        near_message(message, dirs.at[par], res, sdirs.at[par], sres)
    else:
        for i in range(8):
            c = place(OWN, i, odd)
            for h in range(2):
                sol_out[5 * h : 5 * h + 5, i, :] = sol[c, h][0:5]
                res_out[5 * h : 5 * h + 5, i, :] = res[FIRST[OWN] + c, h][0:5]


def moved(cells, pairs):
    return lax.ppermute(cells, "blk", [p for p in pairs(lax.axis_size("blk"))])


def far_pairs(by):
    def pairs(count):
        for i in range(count):
            j = i - by if i % 2 == 0 else i + by
            if 0 <= j < count:
                yield j, i

    return pairs


def chip_pairs(count):
    return [(i, i + 1 - 2 * (i % 2)) for i in range(count)]


def local(kernel, outs, scratch, *args, limit=16 << 20):
    vmem = pl.BlockSpec(memory_space=pltpu.VMEM)
    return pl.pallas_call(
        kernel,
        out_shape=outs,
        in_specs=[vmem] * len(args),
        out_specs=jax.tree.map(lambda _: vmem, outs),
        scratch_shapes=scratch,
        compiler_params=pltpu.CompilerParams(vmem_limit_bytes=limit),
    )(*args)


def inside(x):
    return pltpu.with_memory_space_constraint(x, pltpu.VMEM)


def step(right_side, mean_flow, jac_basis, pattern, shift_diag, dissipation, donors):
    rows, width = right_side.shape[1:]
    f32, bf16 = jnp.float32, jnp.bfloat16
    vmem = pltpu.VMEM
    half = rows * width // 2

    whole, part = local(
        pack_kernel,
        (vmem((FEATS, 2 * half), f32), vmem((FEATS, half), f32)),
        [],
        right_side, mean_flow, pattern, shift_diag, dissipation, donors,
        limit=None,
    )
    far1 = moved(whole, far_pairs(1))
    far2 = moved(part, far_pairs(2))
    near = moved(whole, chip_pairs)
    basis = local(
        basis_kernel, vmem((80, 192), bf16), [vmem((80, LANES), f32)], jac_basis.transpose(1, 2, 0, 3)
    )

    cells = [inside(x) for x in (far2, far1, whole, near)]
    strip = local(strip_kernel, vmem((FEATS, 4 * LANES), f32), [], *cells)
    halo = lax.ppermute(strip, "nrm", [(0, 1), (1, 0)])
    coef, masks, res0, dirs0, parts0, index = local(
        prep_kernel,
        (
            vmem((COLUMNS, 16, WIDTH), f32),
            vmem((COLUMNS, 4, 16, WIDTH), bf16),
            vmem((COLUMNS, 2, 8, WIDTH), f32),
            vmem((SLOTS, 2, 8, WIDTH), f32),
            vmem((SLOTS, 2, 16, WIDTH), bf16),
            vmem((6, 2, 8, LANES), jnp.int32),
        ),
        [],
        *cells,
    )

    halo, basis = inside(halo), inside(basis)
    state = (
        vmem((2, SLOTS, 2, 8, WIDTH), f32),
        vmem((COLUMNS, 2, 8, WIDTH), f32),
        vmem((8, 2, 8, WIDTH), f32),
        vmem((2, 4, 2, 8, LANES), f32),
        vmem((4, 2, 8, LANES), f32),
    )
    scratch = (
        vmem((2, SLOTS, 2, 16, WIDTH), bf16),
        vmem((2, 4, 2, 16, LANES), bf16),
        vmem((4, 8, LANES), f32),
        vmem((4, 2, 8, LANES), jnp.int32),
    )
    *kept, message = local(
        functools.partial(solve_kernel, 0),
        (*state, vmem((16 * (SENT_DIRS + SENT_RES + 1), WIDTH), f32)),
        scratch,
        *[inside(x) for x in (coef, masks, res0, dirs0, parts0, index)], halo, basis,
    )
    message = moved(message, chip_pairs)
    out = jax.ShapeDtypeStruct(right_side.shape, f32)
    return local(
        functools.partial(solve_kernel, MIDDLE), (out, out), (*state, *scratch),
        *[inside(x) for x in (coef, masks, *kept, message, index)], halo, basis,
    )


def solution(mesh):
    return jax.shard_map(
        step,
        mesh=mesh,
        in_specs=(
            P(None, "blk", "nrm"),
            P(None, "blk", "nrm"),
            P(),
            P(None, "blk", "nrm"),
            P("blk", "nrm"),
            P("blk", "nrm"),
            P("blk", None, "nrm"),
        ),
        out_specs=(P(None, "blk", "nrm"), P(None, "blk", "nrm")),
        check_vma=False,
    )
```

```python
import functools

import jax
import jax.numpy as jnp
from jax import lax
from jax.experimental import pallas as pl
from jax.experimental.pallas import tpu as pltpu
from jax.sharding import PartitionSpec as P


ITERS = 6
OMEGA = 0.3
DELTA = 0.9

SHIFT, DAMP, DON0, DON1 = 5, 6, 21, 22
MASK = (7, 13, 14, 15)
FLOW = 16
WHOLE_B, WHOLE_FLOW, WHOLE_DON, WHOLE_ROWS = 128, 256, 336, 344
PART_B, PART_FLOW, PART_DON, PART_ROWS = 64, 128, 148, 152
FEATS = 24
HALO = 16
LANES = 128
WIDTH = 256

FAR2, FAR1, OWN, NEAR = 0, 1, 2, 3
BLOCKS = ((0, 4, 4, 4), (8, 8, 0, 8), (20, 8, 0, 8), (32, 6, 0, 8))
FIRST = (0, 4, 12, 20)
COLUMNS = 26
SLOTS = 38
MIDDLE = 3
FIRST_HALF, EARLY, LATE = 0, 1, 2
PLANS = (
    {
        0: (((0, 2, 1), (1, 0, 4), (2, 0, 4), (3, 0, 2)), (), ()),
        1: (((1, 0, 4), (2, 0, 4), (3, 0, 1)), (1, 2, 3, 4, 5), ()),
        2: (((1, 2, 3), (2, 0, 4)), (2, 3, 4), ()),
    },
    {
        3: (((1, 4, 2), (2, 0, 3)), (2, 3), (1, 2)),
        4: (((1, 6, 1), (2, 0, 2)), (2, 3), (2,)),
        5: (((2, 0, 1),), (3,), ()),
    },
    {
        3: (((2, 6, 1), (3, 0, 2)), (4, 5), (2, 3)),
        4: (((2, 4, 2), (3, 0, 1)), (4, 5), (2,)),
        5: (((2, 2, 3),), (4,), ()),
    },
)
EARLY_LANES = 6 * HALO
TILES = ((0, 1), (1, 0), (1, 1), (2, 0), (2, 1), (3, 0), (3, 1))
TILES_AT = (range(0, 6), range(1, 6), range(1, 5))
FIX = 1 + 3 * (MIDDLE - 1)
LISTS = ((0, 1), (1, 0), (1, 1), (2, 0), (2, 1), (3, 0))
FILLS = ((4, 8, 0), (6, 2, 1), (16, 20, 2), (18, 14, 3), (28, 32, 4), (30, 26, 5))
SENT_DIRS, SENT_RES = 6, 4


def chebyshev():
    sigma = 1.0 / DELTA
    rho = DELTA
    steps = []
    for _ in range(ITERS - 1):
        rho_new = 1.0 / (2.0 * sigma - rho)
        steps.append((rho_new * rho, 2.0 * rho_new / DELTA))
        rho = rho_new
    return steps


def split(full):
    high = full.astype(jnp.bfloat16)
    return high, (full - high.astype(jnp.float32)).astype(jnp.bfloat16)


def precond(pa, pb, a, b):
    return pa * a + pb * b, pa * b - pb * a


def lanes(rows):
    return lax.broadcasted_iota(jnp.int32, (rows, LANES), 1)


def mirrored():
    return lax.rem(lax.axis_index("blk"), 2)


def place(b, c, odd):
    return c if b == FAR2 else c + odd * (7 - 2 * c)


def flow_row(b, c, m, t, odd):
    if b == FAR2:
        return PART_FLOW + 10 * (c - 2) + 2 * m + t if c >= 2 else None
    return WHOLE_FLOW + 8 * (2 * m + t) + place(b, c, odd)


def donor_row(b, side, t, odd):
    if b == FAR2:
        return PART_DON + t
    return WHOLE_DON + 2 * (side + odd * (1 - 2 * side)) + t


def pack_kernel(rhs, flow, mask, shift, damp, donors, whole, part):
    nrm, odd = lax.axis_index("nrm"), mirrored()
    count, width = rhs.shape[1:]
    here = lax.broadcasted_iota(jnp.int32, (1, width), 1) + nrm * width
    offsets = (donors[0] - here).astype(jnp.float32)
    for t in range(2):
        half = slice(t * LANES, (t + 1) * LANES)
        for i in range(count):
            at = 8 * (2 * i + t)
            whole[at : at + 5] = rhs[0:5, i, half]
            whole[at + SHIFT : at + SHIFT + 1] = shift[i : i + 1, half]
            whole[at + DAMP : at + DAMP + 1] = damp[i : i + 1, half]
            whole[at + 7 : at + 8] = mask[0:1, i, half].astype(jnp.float32)
            at = at + WHOLE_B
            whole[at : at + 5] = rhs[5:10, i, half]
            whole[at + 5 : at + 8] = mask[1:4, i, half].astype(jnp.float32)
        for m in range(5):
            at = WHOLE_FLOW + 8 * (2 * m + t)
            whole[at : at + 8] = flow[m, :, half]
        for side in range(2):
            at = WHOLE_DON + 2 * side + t
            whole[at : at + 1] = offsets[side : side + 1, half]
    whole[WHOLE_DON + 4 : WHOLE_ROWS] = jnp.zeros((4, LANES), jnp.float32)
    for c in range(4):
        p = place(OWN, 4 + c, odd)
        for t in range(2):
            for to, base in ((0, 0), (PART_B, WHOLE_B)):
                at = pl.multiple_of(base + 8 * (2 * p + t), 8)
                part[to + 8 * (2 * c + t) : to + 8 * (2 * c + t) + 8] = whole[pl.ds(at, 8)]
            for m in range(5):
                to = flow_row(FAR2, c, m, t, odd)
                if to is not None:
                    part[to : to + 1] = whole[pl.ds(flow_row(OWN, 4 + c, m, t, odd), 1)]
    for t in range(2):
        part[PART_DON + t : PART_DON + t + 1] = whole[pl.ds(donor_row(OWN, 1, t, odd), 1)]
    part[PART_DON + 2 : PART_ROWS] = jnp.zeros((2, LANES), jnp.float32)


def basis_kernel(jac, basis, full):
    full[...] = jnp.zeros(full.shape, jnp.float32)
    for f in range(4):
        for m in range(5):
            for h in range(2):
                for g in range(2):
                    block = jac[m, 5 * h : 5 * h + 5, f, 5 * g : 5 * g + 5]
                    full[16 * m + 8 * h : 16 * m + 8 * h + 5, 16 * f + 8 * g : 16 * f + 8 * g + 5] = block
    j = full[...]
    lane = lanes(80)
    other = jnp.where(lane < 16, pltpu.roll(j, LANES - 16, 1), pltpu.roll(j, 16, 1))
    j = jnp.where((mirrored() == 1) & (lane < 32), other, j)[:, 0:64]
    high, low = split(j)
    basis[:, 0:64] = high
    basis[:, 64:128] = high
    basis[:, 128:192] = low


def strip_kernel(*refs):
    nrm, odd = lax.axis_index("nrm"), mirrored()
    strip = refs[-1]
    lane = lanes(FEATS)
    t = 1 - nrm
    for b, ref in enumerate(refs[:-1]):
        first, sent = BLOCKS[b][2:]
        second = PART_B if b == FAR2 else WHOLE_B
        rows = jnp.zeros((FEATS, LANES), jnp.float32)
        lists = [ref[pl.ds(donor_row(b, side, t, 0), 1)] for side in range(2)]
        for c in range(sent):
            at = 8 * (2 * place(b, c, odd) + t)
            col = first + c
            edge = [ref[pl.ds(pl.multiple_of(base + at, 8), 8)] for base in (0, second)]
            if flow_row(b, c, 0, 0, 0) is None:
                edge.append(jnp.zeros((8, LANES), jnp.float32))
            else:
                flows = [ref[pl.ds(flow_row(b, c, m, t, odd), 1)] for m in range(5)]
                edge.append(jnp.concatenate(flows + lists + [jnp.zeros((1, LANES), jnp.float32)], 0))
            edge = pltpu.roll(jnp.concatenate(edge, 0), lax.rem(HALO * (col + 1 - nrm), LANES), 1)
            rows = jnp.where((lane >= HALO * col) & (lane < HALO * (col + 1)), edge, rows)
        strip[:, b * LANES : (b + 1) * LANES] = rows


def ghosts(src_d, dst_d, dst_h, index, n):
    dst, src, which = FILLS[n]
    lane = lanes(8)
    for c in range(2):
        for t in range(2):
            at = index[which, t]
            across = jnp.abs(at - lane) > LANES // 2
            picked = []
            for h in range(2):
                tiles = [src_d[src + c, h, :, u * LANES : (u + 1) * LANES] for u in (t, 1 - t)]
                here, there = (jnp.take_along_axis(x, at, axis=1) for x in tiles)
                picked.append(jnp.where(across, there, here))
                dst_d[dst + c, h, :, t * LANES : (t + 1) * LANES] = picked[h]
            high, low = split(jnp.concatenate(picked, 0))
            dst_h[dst + c, 0, :, t * LANES : (t + 1) * LANES] = high
            dst_h[dst + c, 1, :, t * LANES : (t + 1) * LANES] = low


def prep_kernel(far2, far1, own, near, coef, masks, res, dirs, parts, index):
    nrm, odd = lax.axis_index("nrm"), mirrored()
    refs = (far2, far1, own, near)
    row = lax.broadcasted_iota(jnp.int32, (8, WIDTH), 0)
    lane = lax.broadcasted_iota(jnp.int32, (16, WIDTH), 1)
    wall = ((lane == 0) & (nrm == 0), (lane == WIDTH - 1) & (nrm == 1))
    for b, ref in enumerate(refs):
        slot, held = BLOCKS[b][:2]
        second = PART_B if b == FAR2 else WHOLE_B
        for c in range(held):
            q, s = FIRST[b] + c, slot + c
            at = 16 * place(b, c, odd)

            def both(row, count, ref=ref, at=at, second=second):
                base = at + (row if row < 8 else second + row - 8)
                if count == 8:
                    base = pl.multiple_of(base, 8)
                return jnp.concatenate([ref[pl.ds(base, count)], ref[pl.ds(base + 8, count)]], 1)

            shift = both(SHIFT, 1)
            scale = 1.0 / (shift * shift + OMEGA * OMEGA)
            pa, pb = shift * scale, OMEGA * scale
            coef[q, 0:1] = shift
            coef[q, 1:2] = both(DAMP, 1)
            coef[q, 2:3] = pa
            coef[q, 3:4] = pb
            for m in range(5):
                for t in range(2):
                    r = flow_row(b, c, m, t, odd)
                    if r is not None:
                        coef[q, 8 + m : 9 + m, t * LANES : (t + 1) * LANES] = ref[pl.ds(r, 1)]
            m = [both(MASK[face], 1) for face in range(4)]
            m[0], m[1] = jnp.where(odd == 1, m[1], m[0]), jnp.where(odd == 1, m[0], m[1])
            for face in range(4):
                wide = jnp.broadcast_to(m[face], (16, WIDTH))
                if face >= 2:
                    wide = jnp.where(wall[face - 2], 0.0, wide)
                masks[q, face] = wide.astype(jnp.bfloat16)
            x = jnp.where(row < 5, both(0, 8), 0.0)
            y = jnp.where(row < 5, both(8, 8), 0.0)
            res[q, 0] = x
            res[q, 1] = y
            dx, dy = precond(pa, pb, x, y)
            dirs[s, 0] = dx
            dirs[s, 1] = dy
            high, low = split(jnp.concatenate([dx, dy], 0))
            parts[s, 0] = high
            parts[s, 1] = low
    for n, (b, side) in enumerate(LISTS):
        for t in range(2):
            offset = refs[b][pl.ds(donor_row(b, side, t, odd), 1)].astype(jnp.int32)
            index[n, t] = jnp.bitwise_and(lanes(8) + offset, LANES - 1)
    for n in range(len(FILLS)):
        ghosts(dirs, dirs, parts, index, n)


def patched(main, tile, c, nrm):
    lane = lax.broadcasted_iota(jnp.int32, (8, WIDTH), 1)
    tile = pltpu.roll(tile, 7 * HALO - 2 * HALO * (c % 4), 1)
    return jnp.where(
        jnp.where(nrm == 0, WIDTH - 1 - lane, lane) < FIX, jnp.concatenate([tile, tile], 1), main
    )


def apply(basis, rows, d, far, shift, damp, flow):
    y = jnp.dot(basis[...], rows, preferred_element_type=jnp.float32)
    out = [shift * d[0] - OMEGA * d[1], shift * d[1] + OMEGA * d[0]]
    for h in range(2):
        out[h] = out[h] + damp * far[h]
    for m in range(5):
        f = flow(m)
        for h in range(2):
            out[h] = out[h] + f * y[16 * m + 8 * h : 16 * m + 8 * h + 8]
    return out


def edge_kernel(
    strip, halo, basis, dirs, res, ed, er, es, sdirs, sres, message, feat, pre, don, cur, rem,
):
    nrm, odd = lax.axis_index("nrm"), mirrored()
    lane = lanes(8)
    wide = lanes(FEATS)
    low_rows = lax.broadcasted_iota(jnp.int32, (8, LANES), 0) < 5
    steps = chebyshev()
    for e, (b, t) in enumerate(TILES):
        at = slice(b * LANES, (b + 1) * LANES)
        mine, theirs = strip[:, at], halo[:, at]
        pair = (jnp.where(nrm == 0, mine, theirs), jnp.where(nrm == 0, theirs, mine))
        from_lane = HALO * (4 * t + jnp.right_shift(lane, 5)) + jnp.bitwise_and(lane, HALO - 1)
        for k in range(3):
            picked = [jnp.take_along_axis(x[8 * k : 8 * k + 8], from_lane, axis=1) for x in pair]
            feat[e, 8 * k : 8 * k + 8] = jnp.where(jnp.bitwise_and(lane, HALO) == 0, *picked)
        shift = feat[e, SHIFT : SHIFT + 1]
        scale = 1.0 / (shift * shift + OMEGA * OMEGA)
        pre[e, 0:1] = shift * scale
        pre[e, 1:2] = OMEGA * scale
        m = [feat[e, MASK[face] : MASK[face] + 1] for face in range(4)]
        pre[e, 2:3] = jnp.where(odd == 1, m[1], m[0])
        pre[e, 3:4] = jnp.where(odd == 1, m[0], m[1])
        pre[e, 4:5] = m[2]
        pre[e, 5:6] = m[3]
        pair = [feat[e, r : r + 1] for r in (DON0, DON1)]
        don[e, 0] = jnp.where(odd == 1, pair[1], pair[0]).astype(jnp.int32) + lane
        don[e, 1] = jnp.where(odd == 1, pair[0], pair[1]).astype(jnp.int32) + lane
        x = [jnp.where(low_rows, feat[e, 8 * h : 8 * h + 8], 0.0) for h in range(2)]
        made = precond(shift * scale, OMEGA * scale, *x)
        for h in range(2):
            rem[e, h] = x[h]
            cur[0, e, h] = made[h]

    span = 2 * HALO
    for step in range(MIDDLE):
        par = step % 2
        for e in TILES_AT[step]:
            b, t = TILES[e]
            rows, far, mid = [[], [], [], []], [], []
            for h in range(2):
                d = cur[par, e, h]
                west, west2 = pltpu.roll(d, span, 1), pltpu.roll(d, 2 * span, 1)
                east, east2 = pltpu.roll(d, LANES - span, 1), pltpu.roll(d, LANES - 2 * span, 1)
                if e > 0:
                    other = cur[par, e - 1, h]
                    if t == 0:
                        close = jnp.take_along_axis(other, jnp.bitwise_and(don[e, 0] + 3 * span, LANES - 1), axis=1)
                        next2 = jnp.take_along_axis(other, jnp.bitwise_and(don[e, 0] + 2 * span, LANES - 1), axis=1)
                    else:
                        close, next2 = pltpu.roll(other, span, 1), pltpu.roll(other, 2 * span, 1)
                    west = jnp.where(lane < span, close, west)
                    west2 = jnp.where(lane < 2 * span, next2, west2)
                if e + 1 < len(TILES):
                    other = cur[par, e + 1, h]
                    if t == 1:
                        close = jnp.take_along_axis(other, jnp.bitwise_and(don[e, 1] + span, LANES - 1), axis=1)
                        next2 = jnp.take_along_axis(other, jnp.bitwise_and(don[e, 1] + 2 * span, LANES - 1), axis=1)
                    else:
                        close, next2 = pltpu.roll(other, LANES - span, 1), pltpu.roll(other, LANES - 2 * span, 1)
                    east = jnp.where(lane >= 3 * span, close, east)
                    east2 = jnp.where(lane >= 2 * span, next2, east2)
                for face, value in enumerate((west, east, pltpu.roll(d, 1, 1), pltpu.roll(d, LANES - 1, 1))):
                    rows[face].append(pre[e, 2 + face : 3 + face] * value)
                far.append(west2 + east2)
                mid.append(d)
            high, low = split(jnp.concatenate(sum(rows, []), 0))
            out = apply(
                basis, jnp.concatenate([high, low, high], 0), mid, far,
                feat[e, SHIFT : SHIFT + 1], feat[e, DAMP : DAMP + 1], lambda m, e=e: feat[e, FLOW + m : FLOW + m + 1],
            )
            new = [rem[e, h] - out[h] for h in range(2)]
            keep, gain = steps[step]
            turned = precond(pre[e, 0:1], pre[e, 1:2], *new)
            for h in range(2):
                rem[e, h] = new[h]
                cur[1 - par, e, h] = keep * mid[h] + gain * turned[h]
                if b == OWN:
                    es[t, h] = mid[h] if step == 0 else es[t, h] + mid[h]

    par = MIDDLE % 2
    from_lane = span * jnp.bitwise_and(jnp.right_shift(lane, 4), 3) + HALO * (1 - nrm) + jnp.bitwise_and(lane, HALO - 1)
    for e in range(1, 5):
        for h in range(2):
            ed[e - 1, h] = cur[par, e, h]
            er[e - 1, h] = rem[e, h]
    for b in (FAR1, OWN):
        for h in range(2):
            for out, tiles in ((sdirs, cur.at[par]), (sres, rem)):
                halves = [jnp.take_along_axis(tiles[2 * b - 1 + t, h], from_lane, axis=1) for t in range(2)]
                out[b - 1, h] = jnp.where(lane < LANES // 2, *halves)

    for n in range(SENT_DIRS):
        c = 7 - n
        for h in range(2):
            at = 8 * (2 * n + h)
            message[at : at + 8, :] = patched(dirs[par, BLOCKS[OWN][0] + c, h], ed[2 + c // 4, h], c, nrm)
    for n in range(SENT_RES):
        c = 7 - n
        for h in range(2):
            at = 16 * SENT_DIRS + 8 * (2 * n + h)
            message[at : at + 8, :] = patched(res[FIRST[OWN] + c, h], er[2 + c // 4, h], c, nrm)
    at = 16 * (SENT_DIRS + SENT_RES)
    for h in range(2):
        message[at + 8 * h : at + 8 * h + 8, 0:LANES] = sdirs[OWN - 1, h]
        message[at + 8 * h : at + 8 * h + 8, LANES:] = sres[OWN - 1, h]


def solve_kernel(phase, *refs):
    if phase == FIRST_HALF:
        (coef, masks, res0, dirs0, parts0, index, basis) = refs[:7]
        (dirs, res, sol, parts) = refs[7:]
    elif phase == EARLY:
        (coef, masks, old_dirs, old_res, old_sol, ed, er, es, old_sdirs, old_sres, index, halo, basis) = refs[:13]
        (dirs, res, sol, parts, kept_dirs, kept_res, sdirs, sres, sparts, spre, sdon) = refs[13:]
    else:
        (coef, masks, _, _, _, _, kept_dirs, kept_res, old_sdirs, old_sres, message, index, halo, basis) = refs[:14]
        (sol_out, res_out, dirs, res, sol, parts, sdirs, sres, sparts, spre, sdon) = refs[14:]
    nrm, odd = lax.axis_index("nrm"), mirrored()
    lane = lanes(8)
    lane16 = lanes(16)
    group = jnp.bitwise_and(lane, HALO - 1)
    low_rows = lax.broadcasted_iota(jnp.int32, (8, LANES), 0) < 5
    steps = chebyshev()

    def dirs_at(step):
        return dirs0 if step == 0 else dirs.at[step % 2]

    def parts_at(step):
        return parts0 if step == 0 else parts.at[step % 2]

    def store(par, s, values):
        for h in range(2):
            dirs[par, s, h] = values[h]
        high, low = split(jnp.concatenate(values, 0))
        parts[par, s, 0] = high
        parts[par, s, 1] = low

    def store_strip(par, b, values):
        for h in range(2):
            sdirs[par, b, h] = values[h]
        high, low = split(jnp.concatenate(values, 0))
        sparts[par, b, 0] = high
        sparts[par, b, 1] = low

    if phase != FIRST_HALF:
        for b in (FAR1, OWN) if phase == EARLY else (OWN, NEAR):
            at = slice(b * LANES, (b + 1) * LANES)
            shift = halo[SHIFT : SHIFT + 1, at]
            scale = 1.0 / (shift * shift + OMEGA * OMEGA)
            spre[b, 0:1] = shift * scale
            spre[b, 1:2] = OMEGA * scale
            m = [halo[MASK[face] : MASK[face] + 1, at] for face in range(4)]
            spre[b, 2:3] = jnp.where(odd == 1, m[1], m[0])
            spre[b, 3:4] = jnp.where(odd == 1, m[0], m[1])
            spre[b, 4:5] = m[2]
            spre[b, 5:6] = m[3]
            pair = [halo[r : r + 1, at] for r in (DON0, DON1)]
            sdon[b, 0] = jnp.where(odd == 1, pair[1], pair[0]).astype(jnp.int32) + lane
            sdon[b, 1] = jnp.where(odd == 1, pair[0], pair[1]).astype(jnp.int32) + lane
        par = MIDDLE % 2
        for b in (FAR1, OWN):
            store_strip(par, b, [old_sdirs[b - 1, h] for h in range(2)])
            for h in range(2):
                sres[b, h] = old_sres[b - 1, h]
    if phase == EARLY:
        blank = [jnp.zeros((8, LANES), jnp.float32)] * 2
        store_strip(0, NEAR, blank)
        store_strip(1, NEAR, blank)
        for b, kept in ((FAR1, range(2, 8)), (OWN, range(8))):
            for c in kept:
                s, q, e = BLOCKS[b][0] + c, FIRST[b] + c, 2 * (b - 1) + c // 4
                store(par, s, [patched(old_dirs[par, s, h], ed[e, h], c, nrm) for h in range(2)])
                for h in range(2):
                    res[q, h] = patched(old_res[q, h], er[e, h], c, nrm)
        for c in range(8):
            for h in range(2):
                sol[c, h] = patched(old_sol[c, h], es[c // 4, h], c, nrm)
    if phase == LATE:
        store_strip(1 - par, FAR1, [kept_dirs[0, h] for h in range(2)])
        slot, first = BLOCKS[NEAR][0], FIRST[NEAR]
        for n in range(SENT_DIRS):
            at = 16 * n
            store(par, slot + n, [message[at + 8 * h : at + 8 * h + 8, :] for h in range(2)])
        for n in range(SENT_RES):
            for h in range(2):
                at = 16 * (SENT_DIRS + n) + 8 * h
                res[first + n, h] = message[at : at + 8, :]
        swap = 7 * HALO - (lane - group) + group
        at = 16 * (SENT_DIRS + SENT_RES)
        values = []
        for h in range(2):
            rows = slice(at + 8 * h, at + 8 * h + 8)
            values.append(jnp.take_along_axis(message[rows, 0:LANES], swap, axis=1))
            sres[NEAR, h] = jnp.take_along_axis(message[rows, LANES:], swap, axis=1)
        store_strip(par, NEAR, values)

    def strips(step):
        par = step % 2
        source = dirs_at(step)
        for b in PLANS[phase][step][2]:
            slot, held, first, _ = BLOCKS[b]
            at = slice(b * LANES, (b + 1) * LANES)
            before, after = sdon[b, 0], sdon[b, 1]
            rows, far, mid = [[], [], [], []], [], []
            for h in range(2):
                d = sdirs[par, b, h]
                edge = jnp.zeros((8, LANES), jnp.float32)
                for c in range(held):
                    col = first + c
                    tile = source[slot + c, h, :, pl.ds(pl.multiple_of((1 - nrm) * LANES, LANES), LANES)]
                    tile = pltpu.roll(tile, HALO * col + 1 + 14 * nrm, 1)
                    edge = jnp.where((lane >= HALO * col) & (lane < HALO * (col + 1)), tile, edge)
                west, west2 = pltpu.roll(d, HALO, 1), pltpu.roll(d, 2 * HALO, 1)
                east, east2 = pltpu.roll(d, LANES - HALO, 1), pltpu.roll(d, LANES - 2 * HALO, 1)
                if b > 1:
                    other = sdirs[par, b - 1, h]
                    close = jnp.take_along_axis(other, jnp.bitwise_and(before + 7 * HALO, LANES - 1), axis=1)
                    next2 = jnp.take_along_axis(other, jnp.bitwise_and(before + 6 * HALO, LANES - 1), axis=1)
                    west = jnp.where(lane < HALO, close, west)
                    west2 = jnp.where(lane < 2 * HALO, next2, west2)
                if b < 3:
                    other = sdirs[par, b + 1, h]
                    close = jnp.take_along_axis(other, jnp.bitwise_and(after + HALO, LANES - 1), axis=1)
                    next2 = jnp.take_along_axis(other, jnp.bitwise_and(after + 2 * HALO, LANES - 1), axis=1)
                    east = jnp.where(lane >= 7 * HALO, close, east)
                    east2 = jnp.where(lane >= 6 * HALO, next2, east2)
                south = jnp.where(group == 0, edge, pltpu.roll(d, 1, 1))
                north = jnp.where(group == HALO - 1, edge, pltpu.roll(d, LANES - 1, 1))
                for face, value in enumerate((west, east, south, north)):
                    rows[face].append(spre[b, 2 + face : 3 + face] * value)
                far.append(west2 + east2)
                mid.append(d)
            high, low = split(jnp.concatenate(sum(rows, []), 0))
            out = apply(
                basis, jnp.concatenate([high, low, high], 0), mid, far, halo[SHIFT : SHIFT + 1, at], halo[DAMP : DAMP + 1, at],
                lambda m, at=at: halo[FLOW + m : FLOW + m + 1, at],
            )
            new = [sres[b, h] - out[h] for h in range(2)]
            keep, gain = steps[step]
            turned = precond(spre[b, 0:1], spre[b, 1:2], *new)
            made = [keep * mid[h] + gain * turned[h] for h in range(2)]
            if phase == LATE and b == OWN and step == MIDDLE:
                done = lane < EARLY_LANES
                new = [jnp.where(done, kept_res[h], new[h]) for h in range(2)]
                made = [jnp.where(done, kept_dirs[1, h], made[h]) for h in range(2)]
            for h in range(2):
                sres[b, h] = new[h]
                if phase == EARLY and step == MIDDLE:
                    kept_dirs[b - 1, h] = made[h]
                    if b == OWN:
                        kept_res[h] = new[h]
            store_strip(1 - par, b, made)

    def column(step, b, c):
        slot, _, first, _ = BLOCKS[b]
        s, q = slot + c, FIRST[b] + c
        par = step % 2
        p = parts_at(step)
        turn = 127 - 14 * nrm - HALO * (first + c)
        stack = [[], []]
        for k in range(2):
            tiles = [p[s, k, :, t * LANES : (t + 1) * LANES] for t in range(2)]
            up = [pltpu.roll(x, 1, 1) for x in tiles]
            down = [pltpu.roll(x, LANES - 1, 1) for x in tiles]
            south = [up[0], jnp.where(lane16 == 0, up[0], up[1])]
            north = [jnp.where(lane16 == LANES - 1, down[1], down[0]), down[1]]
            if phase != FIRST_HALF:
                edge = pltpu.roll(sparts[par, b, k], turn, 1)
                south[0] = jnp.where(lane16 == 0, edge, south[0])
                north[1] = jnp.where(lane16 == LANES - 1, edge, north[1])
            for face, value in enumerate(
                (p[s - 1, k], p[s + 1, k], jnp.concatenate(south, 1), jnp.concatenate(north, 1))
            ):
                stack[k].append(masks[q, face] * value)
        return jnp.concatenate(stack[0] + stack[1] + stack[0], 0)

    def finish(step, b, c, rows):
        s, q = BLOCKS[b][0] + c, FIRST[b] + c
        d = dirs_at(step)
        mid = [d[s, h] for h in range(2)]
        far = [d[s - 2, h] + d[s + 2, h] for h in range(2)]
        out = apply(basis, rows, mid, far, coef[q, 0:1], coef[q, 1:2], lambda m: coef[q, 8 + m : 9 + m])
        old = res0 if step == 0 else res
        new = [old[q, h] - out[h] for h in range(2)]
        for h in range(2):
            res[q, h] = new[h]
            if b == OWN:
                sol[c, h] = mid[h] if step == 0 else sol[c, h] + mid[h]
        if step + 1 < ITERS:
            keep, gain = steps[step]
            turned = precond(coef[q, 2:3], coef[q, 3:4], *new)
            store(1 - step % 2, s, [keep * mid[h] + gain * turned[h] for h in range(2)])

    for step, (columns, fills, _) in PLANS[phase].items():
        par = step % 2
        for n in fills:
            ghosts(dirs.at[par], dirs.at[par], parts.at[par], index, n)
        strips(step)
        for b, start, pairs in columns:
            for c in range(start, start + 2 * pairs):
                finish(step, b, c, column(step, b, c))

    if phase == LATE:
        for i in range(8):
            c = place(OWN, i, odd)
            for h in range(2):
                sol_out[5 * h : 5 * h + 5, i, :] = sol[c, h][0:5]
                res_out[5 * h : 5 * h + 5, i, :] = res[FIRST[OWN] + c, h][0:5]


def moved(cells, pairs):
    return lax.ppermute(cells, "blk", [p for p in pairs(lax.axis_size("blk"))])


def far_pairs(by):
    def pairs(count):
        for i in range(count):
            j = i - by if i % 2 == 0 else i + by
            if 0 <= j < count:
                yield j, i

    return pairs


def chip_pairs(count):
    return [(i, i + 1 - 2 * (i % 2)) for i in range(count)]


def local(kernel, outs, scratch, *args, limit=16 << 20, aliases=None):
    vmem = pl.BlockSpec(memory_space=pltpu.VMEM)
    return pl.pallas_call(
        kernel,
        out_shape=outs,
        in_specs=[vmem] * len(args),
        out_specs=jax.tree.map(lambda _: vmem, outs),
        scratch_shapes=scratch,
        input_output_aliases=aliases or {},
        compiler_params=pltpu.CompilerParams(vmem_limit_bytes=limit),
    )(*args)


def inside(x):
    return pltpu.with_memory_space_constraint(x, pltpu.VMEM)


def step(right_side, mean_flow, jac_basis, pattern, shift_diag, dissipation, donors):
    f32, bf16 = jnp.float32, jnp.bfloat16
    vmem = pltpu.VMEM

    whole, part = local(
        pack_kernel,
        (vmem((WHOLE_ROWS, LANES), f32), vmem((PART_ROWS, LANES), f32)),
        [],
        right_side, mean_flow, pattern, shift_diag, dissipation, donors,
        limit=None,
    )
    far1 = moved(whole, far_pairs(1))
    far2 = moved(part, far_pairs(2))
    near = moved(whole, chip_pairs)
    basis = local(
        basis_kernel, vmem((80, 192), bf16), [vmem((80, LANES), f32)], jac_basis.transpose(1, 2, 0, 3)
    )

    cells = [inside(x) for x in (far2, far1, whole, near)]
    strip = local(strip_kernel, vmem((FEATS, 4 * LANES), f32), [], *cells)
    halo = lax.ppermute(strip, "nrm", [(0, 1), (1, 0)])
    coef, masks, res0, dirs0, parts0, index = local(
        prep_kernel,
        (
            vmem((COLUMNS, 16, WIDTH), f32),
            vmem((COLUMNS, 4, 16, WIDTH), bf16),
            vmem((COLUMNS, 2, 8, WIDTH), f32),
            vmem((SLOTS, 2, 8, WIDTH), f32),
            vmem((SLOTS, 2, 16, WIDTH), bf16),
            vmem((6, 2, 8, LANES), jnp.int32),
        ),
        [],
        *cells,
    )

    basis = inside(basis)
    fixed = [inside(x) for x in (coef, masks)]
    index = inside(index)
    state = (
        vmem((2, SLOTS, 2, 8, WIDTH), f32),
        vmem((COLUMNS, 2, 8, WIDTH), f32),
        vmem((8, 2, 8, WIDTH), f32),
    )
    parts = vmem((2, SLOTS, 2, 16, WIDTH), bf16)
    dirs, res, sol = local(
        functools.partial(solve_kernel, FIRST_HALF), state, (parts,),
        *fixed, *[inside(x) for x in (res0, dirs0, parts0)], index, basis,
    )
    dirs, res, halo = inside(dirs), inside(res), inside(halo)
    *edges, message = local(
        edge_kernel,
        (
            vmem((4, 2, 8, LANES), f32),
            vmem((4, 2, 8, LANES), f32),
            vmem((2, 2, 8, LANES), f32),
            vmem((2, 2, 8, LANES), f32),
            vmem((2, 2, 8, LANES), f32),
            vmem((16 * (SENT_DIRS + SENT_RES + 1), WIDTH), f32),
        ),
        (
            vmem((7, FEATS, LANES), f32),
            vmem((7, 8, LANES), f32),
            vmem((7, 2, 8, LANES), jnp.int32),
            vmem((2, 7, 2, 8, LANES), f32),
            vmem((7, 2, 8, LANES), f32),
        ),
        inside(strip), halo, basis, dirs, res,
    )
    message = moved(message, chip_pairs)
    scratch = (
        vmem((2, 4, 2, 8, LANES), f32),
        vmem((4, 2, 8, LANES), f32),
        vmem((2, 4, 2, 16, LANES), bf16),
        vmem((4, 8, LANES), f32),
        vmem((4, 2, 8, LANES), jnp.int32),
    )
    edges = [inside(x) for x in edges]
    kept = local(
        functools.partial(solve_kernel, EARLY),
        (*state, parts, vmem((2, 2, 8, LANES), f32), vmem((2, 8, LANES), f32)),
        scratch,
        *fixed, dirs, res, inside(sol), *edges, index, halo, basis,
    )
    out = jax.ShapeDtypeStruct(right_side.shape, f32)
    return local(
        functools.partial(solve_kernel, LATE), (out, out, *state, parts), scratch,
        *fixed, *[inside(x) for x in kept], *edges[3:], inside(message), index, halo, basis,
        aliases={2: 2, 3: 3, 4: 4, 5: 5},
    )[:2]


def solution(mesh):
    return jax.shard_map(
        step,
        mesh=mesh,
        in_specs=(
            P(None, "blk", "nrm"),
            P(None, "blk", "nrm"),
            P(),
            P(None, "blk", "nrm"),
            P("blk", "nrm"),
            P("blk", "nrm"),
            P("blk", None, "nrm"),
        ),
        out_specs=(P(None, "blk", "nrm"), P(None, "blk", "nrm")),
        check_vma=False,
    )
```

```python
import functools

import jax
import jax.numpy as jnp
from jax import lax
from jax.experimental import pallas as pl
from jax.experimental.pallas import tpu as pltpu
from jax.sharding import PartitionSpec as P


ITERS = 6
OMEGA = 0.3
DELTA = 0.9

SHIFT, DAMP, DON0, DON1 = 5, 6, 21, 22
MASK = (7, 13, 14, 15)
FLOW = 16
WHOLE_B, WHOLE_FLOW, WHOLE_DON, WHOLE_ROWS = 128, 256, 336, 344
PART_B, PART_FLOW, PART_DON, PART_ROWS = 64, 128, 148, 152
FEATS = 24
HALO = 16
LANES = 128
WIDTH = 256

FAR2, FAR1, OWN, NEAR = 0, 1, 2, 3
BLOCKS = ((0, 4, 4, 4), (8, 8, 0, 8), (20, 8, 0, 8), (32, 6, 0, 8))
FIRST = (0, 4, 12, 20)
COLUMNS = 26
SLOTS = 38
MIDDLE = 3
FIRST_HALF, EARLY, LATE = 0, 1, 2
PLANS = (
    {
        0: (((0, 2, 1), (1, 0, 4), (2, 0, 4), (3, 0, 2)), (), ()),
        1: (((1, 0, 4), (2, 0, 4), (3, 0, 1)), (1, 2, 3, 4, 5), ()),
        2: (((1, 2, 3), (2, 0, 4)), (2, 3, 4), ()),
    },
    {
        3: (((1, 4, 2), (2, 0, 3)), (2, 3), (1, 2)),
        4: (((1, 6, 1), (2, 0, 2)), (2, 3), (2,)),
        5: (((2, 0, 1),), (3,), ()),
    },
    {
        3: (((2, 6, 1), (3, 0, 2)), (4, 5), (2, 3)),
        4: (((2, 4, 2), (3, 0, 1)), (4, 5), (2,)),
        5: (((2, 2, 3),), (4,), ()),
    },
)
EARLY_LANES = 6 * HALO
TILES = ((0, 1), (1, 0), (1, 1), (2, 0), (2, 1), (3, 0), (3, 1))
TILES_AT = (range(0, 6), range(1, 6), range(1, 5))
FIX = 1 + 3 * (MIDDLE - 1)
LISTS = ((0, 1), (1, 0), (1, 1), (2, 0), (2, 1), (3, 0))
FILLS = ((4, 8, 0), (6, 2, 1), (16, 20, 2), (18, 14, 3), (28, 32, 4), (30, 26, 5))
SENT_DIRS, SENT_RES = 6, 4


def chebyshev():
    sigma = 1.0 / DELTA
    rho = DELTA
    steps = []
    for _ in range(ITERS - 1):
        rho_new = 1.0 / (2.0 * sigma - rho)
        steps.append((rho_new * rho, 2.0 * rho_new / DELTA))
        rho = rho_new
    return steps


def split(full):
    high = full.astype(jnp.bfloat16)
    return high, (full - high.astype(jnp.float32)).astype(jnp.bfloat16)


def precond(pa, pb, a, b):
    return pa * a + pb * b, pa * b - pb * a


def lanes(rows):
    return lax.broadcasted_iota(jnp.int32, (rows, LANES), 1)


def mirrored():
    return lax.rem(lax.axis_index("blk"), 2)


def place(b, c, odd):
    return c if b == FAR2 else c + odd * (7 - 2 * c)


def flow_row(b, c, m, t, odd):
    if b == FAR2:
        return PART_FLOW + 10 * (c - 2) + 2 * m + t if c >= 2 else None
    return WHOLE_FLOW + 8 * (2 * m + t) + place(b, c, odd)


def donor_row(b, side, t, odd):
    if b == FAR2:
        return PART_DON + t
    return WHOLE_DON + 2 * (side + odd * (1 - 2 * side)) + t


def pack_kernel(rhs, flow, mask, shift, damp, donors, whole, part):
    nrm, odd = lax.axis_index("nrm"), mirrored()
    count, width = rhs.shape[1:]
    here = lax.broadcasted_iota(jnp.int32, (1, width), 1) + nrm * width
    offsets = (donors[0] - here).astype(jnp.float32)
    for t in range(2):
        half = slice(t * LANES, (t + 1) * LANES)
        for i in range(count):
            at = 8 * (2 * i + t)
            whole[at : at + 5] = rhs[0:5, i, half]
            whole[at + SHIFT : at + SHIFT + 1] = shift[i : i + 1, half]
            whole[at + DAMP : at + DAMP + 1] = damp[i : i + 1, half]
            whole[at + 7 : at + 8] = mask[0:1, i, half].astype(jnp.float32)
            at = at + WHOLE_B
            whole[at : at + 5] = rhs[5:10, i, half]
            whole[at + 5 : at + 8] = mask[1:4, i, half].astype(jnp.float32)
        for m in range(5):
            at = WHOLE_FLOW + 8 * (2 * m + t)
            whole[at : at + 8] = flow[m, :, half]
        for side in range(2):
            at = WHOLE_DON + 2 * side + t
            whole[at : at + 1] = offsets[side : side + 1, half]
    whole[WHOLE_DON + 4 : WHOLE_ROWS] = jnp.zeros((4, LANES), jnp.float32)
    for c in range(4):
        p = place(OWN, 4 + c, odd)
        for t in range(2):
            for to, base in ((0, 0), (PART_B, WHOLE_B)):
                at = pl.multiple_of(base + 8 * (2 * p + t), 8)
                part[to + 8 * (2 * c + t) : to + 8 * (2 * c + t) + 8] = whole[pl.ds(at, 8)]
            for m in range(5):
                to = flow_row(FAR2, c, m, t, odd)
                if to is not None:
                    part[to : to + 1] = whole[pl.ds(flow_row(OWN, 4 + c, m, t, odd), 1)]
    for t in range(2):
        part[PART_DON + t : PART_DON + t + 1] = whole[pl.ds(donor_row(OWN, 1, t, odd), 1)]
    part[PART_DON + 2 : PART_ROWS] = jnp.zeros((2, LANES), jnp.float32)


def basis_kernel(jac, basis, full):
    full[...] = jnp.zeros(full.shape, jnp.float32)
    for f in range(4):
        for m in range(5):
            for h in range(2):
                for g in range(2):
                    block = jac[m, 5 * h : 5 * h + 5, f, 5 * g : 5 * g + 5]
                    full[16 * m + 8 * h : 16 * m + 8 * h + 5, 16 * f + 8 * g : 16 * f + 8 * g + 5] = block
    j = full[...]
    lane = lanes(80)
    other = jnp.where(lane < 16, pltpu.roll(j, LANES - 16, 1), pltpu.roll(j, 16, 1))
    j = jnp.where((mirrored() == 1) & (lane < 32), other, j)[:, 0:64]
    high, low = split(j)
    basis[:, 0:64] = high
    basis[:, 64:128] = high
    basis[:, 128:192] = low


def strip_kernel(blocks, *refs):
    nrm, odd = lax.axis_index("nrm"), mirrored()
    strip = refs[-1]
    lane = lanes(FEATS)
    t = 1 - nrm
    if len(blocks) == 1:
        strip[...] = refs[0][...]
    for b, ref in zip(blocks, refs[-1 - len(blocks) : -1], strict=True):
        first, sent = BLOCKS[b][2:]
        second = PART_B if b == FAR2 else WHOLE_B
        rows = jnp.zeros((FEATS, LANES), jnp.float32)
        lists = [ref[pl.ds(donor_row(b, side, t, 0), 1)] for side in range(2)]
        for c in range(sent):
            at = 8 * (2 * place(b, c, odd) + t)
            col = first + c
            edge = [ref[pl.ds(pl.multiple_of(base + at, 8), 8)] for base in (0, second)]
            if flow_row(b, c, 0, 0, 0) is None:
                edge.append(jnp.zeros((8, LANES), jnp.float32))
            else:
                flows = [ref[pl.ds(flow_row(b, c, m, t, odd), 1)] for m in range(5)]
                edge.append(jnp.concatenate(flows + lists + [jnp.zeros((1, LANES), jnp.float32)], 0))
            edge = pltpu.roll(jnp.concatenate(edge, 0), lax.rem(HALO * (col + 1 - nrm), LANES), 1)
            rows = jnp.where((lane >= HALO * col) & (lane < HALO * (col + 1)), edge, rows)
        strip[:, b * LANES : (b + 1) * LANES] = rows


def ghosts(src_d, dst_d, dst_h, index, n):
    dst, src, which = FILLS[n]
    lane = lanes(8)
    for c in range(2):
        for t in range(2):
            at = index[which, t]
            across = jnp.abs(at - lane) > LANES // 2
            picked = []
            for h in range(2):
                tiles = [src_d[src + c, h, :, u * LANES : (u + 1) * LANES] for u in (t, 1 - t)]
                here, there = (jnp.take_along_axis(x, at, axis=1) for x in tiles)
                picked.append(jnp.where(across, there, here))
                dst_d[dst + c, h, :, t * LANES : (t + 1) * LANES] = picked[h]
            high, low = split(jnp.concatenate(picked, 0))
            dst_h[dst + c, 0, :, t * LANES : (t + 1) * LANES] = high
            dst_h[dst + c, 1, :, t * LANES : (t + 1) * LANES] = low


def prep_kernel(far2, far1, own, near, coef, masks, res, dirs, parts, index):
    nrm, odd = lax.axis_index("nrm"), mirrored()
    refs = (far2, far1, own, near)
    row = lax.broadcasted_iota(jnp.int32, (8, WIDTH), 0)
    lane = lax.broadcasted_iota(jnp.int32, (16, WIDTH), 1)
    wall = ((lane == 0) & (nrm == 0), (lane == WIDTH - 1) & (nrm == 1))
    for b, ref in enumerate(refs):
        slot, held = BLOCKS[b][:2]
        second = PART_B if b == FAR2 else WHOLE_B
        for c in range(held):
            q, s = FIRST[b] + c, slot + c
            at = 16 * place(b, c, odd)

            def both(row, count, ref=ref, at=at, second=second):
                base = at + (row if row < 8 else second + row - 8)
                if count == 8:
                    base = pl.multiple_of(base, 8)
                return jnp.concatenate([ref[pl.ds(base, count)], ref[pl.ds(base + 8, count)]], 1)

            shift = both(SHIFT, 1)
            scale = 1.0 / (shift * shift + OMEGA * OMEGA)
            pa, pb = shift * scale, OMEGA * scale
            coef[q, 0:1] = shift
            coef[q, 1:2] = both(DAMP, 1)
            coef[q, 2:3] = pa
            coef[q, 3:4] = pb
            for m in range(5):
                for t in range(2):
                    r = flow_row(b, c, m, t, odd)
                    if r is not None:
                        coef[q, 8 + m : 9 + m, t * LANES : (t + 1) * LANES] = ref[pl.ds(r, 1)]
            m = [both(MASK[face], 1) for face in range(4)]
            m[0], m[1] = jnp.where(odd == 1, m[1], m[0]), jnp.where(odd == 1, m[0], m[1])
            for face in range(4):
                wide = jnp.broadcast_to(m[face], (16, WIDTH))
                if face >= 2:
                    wide = jnp.where(wall[face - 2], 0.0, wide)
                masks[q, face] = wide.astype(jnp.bfloat16)
            x = jnp.where(row < 5, both(0, 8), 0.0)
            y = jnp.where(row < 5, both(8, 8), 0.0)
            res[q, 0] = x
            res[q, 1] = y
            dx, dy = precond(pa, pb, x, y)
            dirs[s, 0] = dx
            dirs[s, 1] = dy
            high, low = split(jnp.concatenate([dx, dy], 0))
            parts[s, 0] = high
            parts[s, 1] = low
    for n, (b, side) in enumerate(LISTS):
        for t in range(2):
            offset = refs[b][pl.ds(donor_row(b, side, t, odd), 1)].astype(jnp.int32)
            index[n, t] = jnp.bitwise_and(lanes(8) + offset, LANES - 1)
    for n in range(len(FILLS)):
        ghosts(dirs, dirs, parts, index, n)


def patched(main, tile, c, nrm):
    lane = lax.broadcasted_iota(jnp.int32, (8, WIDTH), 1)
    tile = pltpu.roll(tile, 7 * HALO - 2 * HALO * (c % 4), 1)
    return jnp.where(
        jnp.where(nrm == 0, WIDTH - 1 - lane, lane) < FIX, jnp.concatenate([tile, tile], 1), main
    )


def apply(basis, rows, d, far, shift, damp, flow):
    y = jnp.dot(basis[...], rows, preferred_element_type=jnp.float32)
    out = [shift * d[0] - OMEGA * d[1], shift * d[1] + OMEGA * d[0]]
    for h in range(2):
        out[h] = out[h] + damp * far[h]
    for m in range(5):
        f = flow(m)
        for h in range(2):
            out[h] = out[h] + f * y[16 * m + 8 * h : 16 * m + 8 * h + 8]
    return out


def edge_kernel(
    strip, halo, basis, dirs, res, ed, er, es, sdirs, sres, message, feat, pre, don, cur, rem,
):
    nrm, odd = lax.axis_index("nrm"), mirrored()
    lane = lanes(8)
    wide = lanes(FEATS)
    low_rows = lax.broadcasted_iota(jnp.int32, (8, LANES), 0) < 5
    steps = chebyshev()
    for e, (b, t) in enumerate(TILES):
        at = slice(b * LANES, (b + 1) * LANES)
        mine, theirs = strip[:, at], halo[:, at]
        pair = (jnp.where(nrm == 0, mine, theirs), jnp.where(nrm == 0, theirs, mine))
        from_lane = HALO * (4 * t + jnp.right_shift(lane, 5)) + jnp.bitwise_and(lane, HALO - 1)
        for k in range(3):
            picked = [jnp.take_along_axis(x[8 * k : 8 * k + 8], from_lane, axis=1) for x in pair]
            feat[e, 8 * k : 8 * k + 8] = jnp.where(jnp.bitwise_and(lane, HALO) == 0, *picked)
        shift = feat[e, SHIFT : SHIFT + 1]
        scale = 1.0 / (shift * shift + OMEGA * OMEGA)
        pre[e, 0:1] = shift * scale
        pre[e, 1:2] = OMEGA * scale
        m = [feat[e, MASK[face] : MASK[face] + 1] for face in range(4)]
        pre[e, 2:3] = jnp.where(odd == 1, m[1], m[0])
        pre[e, 3:4] = jnp.where(odd == 1, m[0], m[1])
        pre[e, 4:5] = m[2]
        pre[e, 5:6] = m[3]
        pair = [feat[e, r : r + 1] for r in (DON0, DON1)]
        don[e, 0] = jnp.where(odd == 1, pair[1], pair[0]).astype(jnp.int32) + lane
        don[e, 1] = jnp.where(odd == 1, pair[0], pair[1]).astype(jnp.int32) + lane
        x = [jnp.where(low_rows, feat[e, 8 * h : 8 * h + 8], 0.0) for h in range(2)]
        made = precond(shift * scale, OMEGA * scale, *x)
        for h in range(2):
            rem[e, h] = x[h]
            cur[0, e, h] = made[h]

    span = 2 * HALO
    for step in range(MIDDLE):
        par = step % 2
        for e in TILES_AT[step]:
            b, t = TILES[e]
            rows, far, mid = [[], [], [], []], [], []
            for h in range(2):
                d = cur[par, e, h]
                west, west2 = pltpu.roll(d, span, 1), pltpu.roll(d, 2 * span, 1)
                east, east2 = pltpu.roll(d, LANES - span, 1), pltpu.roll(d, LANES - 2 * span, 1)
                if e > 0:
                    other = cur[par, e - 1, h]
                    if t == 0:
                        close = jnp.take_along_axis(other, jnp.bitwise_and(don[e, 0] + 3 * span, LANES - 1), axis=1)
                        next2 = jnp.take_along_axis(other, jnp.bitwise_and(don[e, 0] + 2 * span, LANES - 1), axis=1)
                    else:
                        close, next2 = pltpu.roll(other, span, 1), pltpu.roll(other, 2 * span, 1)
                    west = jnp.where(lane < span, close, west)
                    west2 = jnp.where(lane < 2 * span, next2, west2)
                if e + 1 < len(TILES):
                    other = cur[par, e + 1, h]
                    if t == 1:
                        close = jnp.take_along_axis(other, jnp.bitwise_and(don[e, 1] + span, LANES - 1), axis=1)
                        next2 = jnp.take_along_axis(other, jnp.bitwise_and(don[e, 1] + 2 * span, LANES - 1), axis=1)
                    else:
                        close, next2 = pltpu.roll(other, LANES - span, 1), pltpu.roll(other, LANES - 2 * span, 1)
                    east = jnp.where(lane >= 3 * span, close, east)
                    east2 = jnp.where(lane >= 2 * span, next2, east2)
                for face, value in enumerate((west, east, pltpu.roll(d, 1, 1), pltpu.roll(d, LANES - 1, 1))):
                    rows[face].append(pre[e, 2 + face : 3 + face] * value)
                far.append(west2 + east2)
                mid.append(d)
            high, low = split(jnp.concatenate(sum(rows, []), 0))
            out = apply(
                basis, jnp.concatenate([high, low, high], 0), mid, far,
                feat[e, SHIFT : SHIFT + 1], feat[e, DAMP : DAMP + 1], lambda m, e=e: feat[e, FLOW + m : FLOW + m + 1],
            )
            new = [rem[e, h] - out[h] for h in range(2)]
            keep, gain = steps[step]
            turned = precond(pre[e, 0:1], pre[e, 1:2], *new)
            for h in range(2):
                rem[e, h] = new[h]
                cur[1 - par, e, h] = keep * mid[h] + gain * turned[h]
                if b == OWN:
                    es[t, h] = mid[h] if step == 0 else es[t, h] + mid[h]

    par = MIDDLE % 2
    from_lane = span * jnp.bitwise_and(jnp.right_shift(lane, 4), 3) + HALO * (1 - nrm) + jnp.bitwise_and(lane, HALO - 1)
    for e in range(1, 5):
        for h in range(2):
            ed[e - 1, h] = cur[par, e, h]
            er[e - 1, h] = rem[e, h]
    for b in (FAR1, OWN):
        for h in range(2):
            for out, tiles in ((sdirs, cur.at[par]), (sres, rem)):
                halves = [jnp.take_along_axis(tiles[2 * b - 1 + t, h], from_lane, axis=1) for t in range(2)]
                out[b - 1, h] = jnp.where(lane < LANES // 2, *halves)

    for n in range(SENT_DIRS):
        c = 7 - n
        for h in range(2):
            at = 8 * (2 * n + h)
            message[at : at + 8, :] = patched(dirs[par, BLOCKS[OWN][0] + c, h], ed[2 + c // 4, h], c, nrm)
    for n in range(SENT_RES):
        c = 7 - n
        for h in range(2):
            at = 16 * SENT_DIRS + 8 * (2 * n + h)
            message[at : at + 8, :] = patched(res[FIRST[OWN] + c, h], er[2 + c // 4, h], c, nrm)
    at = 16 * (SENT_DIRS + SENT_RES)
    for h in range(2):
        message[at + 8 * h : at + 8 * h + 8, 0:LANES] = sdirs[OWN - 1, h]
        message[at + 8 * h : at + 8 * h + 8, LANES:] = sres[OWN - 1, h]


def solve_kernel(phase, *refs):
    if phase == FIRST_HALF:
        (coef, masks, res0, dirs0, parts0, index, basis) = refs[:7]
        (dirs, res, sol, parts) = refs[7:]
    elif phase == EARLY:
        (coef, masks, old_dirs, old_res, old_sol, ed, er, es, old_sdirs, old_sres, index, halo, basis) = refs[:13]
        (dirs, res, sol, parts, kept_dirs, kept_res, sdirs, sres, sparts, spre, sdon) = refs[13:]
    else:
        (coef, masks, _, _, _, _, kept_dirs, kept_res, old_sdirs, old_sres, message, index, halo, basis) = refs[:14]
        (sol_out, res_out, dirs, res, sol, parts, sdirs, sres, sparts, spre, sdon) = refs[14:]
    nrm, odd = lax.axis_index("nrm"), mirrored()
    lane = lanes(8)
    lane16 = lanes(16)
    group = jnp.bitwise_and(lane, HALO - 1)
    low_rows = lax.broadcasted_iota(jnp.int32, (8, LANES), 0) < 5
    steps = chebyshev()

    def dirs_at(step):
        return dirs0 if step == 0 else dirs.at[step % 2]

    def parts_at(step):
        return parts0 if step == 0 else parts.at[step % 2]

    def store(par, s, values):
        for h in range(2):
            dirs[par, s, h] = values[h]
        high, low = split(jnp.concatenate(values, 0))
        parts[par, s, 0] = high
        parts[par, s, 1] = low

    def store_strip(par, b, values):
        for h in range(2):
            sdirs[par, b, h] = values[h]
        high, low = split(jnp.concatenate(values, 0))
        sparts[par, b, 0] = high
        sparts[par, b, 1] = low

    if phase != FIRST_HALF:
        for b in (FAR1, OWN) if phase == EARLY else (OWN, NEAR):
            at = slice(b * LANES, (b + 1) * LANES)
            shift = halo[SHIFT : SHIFT + 1, at]
            scale = 1.0 / (shift * shift + OMEGA * OMEGA)
            spre[b, 0:1] = shift * scale
            spre[b, 1:2] = OMEGA * scale
            m = [halo[MASK[face] : MASK[face] + 1, at] for face in range(4)]
            spre[b, 2:3] = jnp.where(odd == 1, m[1], m[0])
            spre[b, 3:4] = jnp.where(odd == 1, m[0], m[1])
            spre[b, 4:5] = m[2]
            spre[b, 5:6] = m[3]
            pair = [halo[r : r + 1, at] for r in (DON0, DON1)]
            sdon[b, 0] = jnp.where(odd == 1, pair[1], pair[0]).astype(jnp.int32) + lane
            sdon[b, 1] = jnp.where(odd == 1, pair[0], pair[1]).astype(jnp.int32) + lane
        par = MIDDLE % 2
        for b in (FAR1, OWN):
            store_strip(par, b, [old_sdirs[b - 1, h] for h in range(2)])
            for h in range(2):
                sres[b, h] = old_sres[b - 1, h]
    if phase == EARLY:
        blank = [jnp.zeros((8, LANES), jnp.float32)] * 2
        store_strip(0, NEAR, blank)
        store_strip(1, NEAR, blank)
        for b, kept in ((FAR1, range(2, 8)), (OWN, range(8))):
            for c in kept:
                s, q, e = BLOCKS[b][0] + c, FIRST[b] + c, 2 * (b - 1) + c // 4
                store(par, s, [patched(old_dirs[par, s, h], ed[e, h], c, nrm) for h in range(2)])
                for h in range(2):
                    res[q, h] = patched(old_res[q, h], er[e, h], c, nrm)
        for c in range(8):
            for h in range(2):
                sol[c, h] = patched(old_sol[c, h], es[c // 4, h], c, nrm)
    if phase == LATE:
        store_strip(1 - par, FAR1, [kept_dirs[0, h] for h in range(2)])
        slot, first = BLOCKS[NEAR][0], FIRST[NEAR]
        for n in range(SENT_DIRS):
            at = 16 * n
            store(par, slot + n, [message[at + 8 * h : at + 8 * h + 8, :] for h in range(2)])
        for n in range(SENT_RES):
            for h in range(2):
                at = 16 * (SENT_DIRS + n) + 8 * h
                res[first + n, h] = message[at : at + 8, :]
        swap = 7 * HALO - (lane - group) + group
        at = 16 * (SENT_DIRS + SENT_RES)
        values = []
        for h in range(2):
            rows = slice(at + 8 * h, at + 8 * h + 8)
            values.append(jnp.take_along_axis(message[rows, 0:LANES], swap, axis=1))
            sres[NEAR, h] = jnp.take_along_axis(message[rows, LANES:], swap, axis=1)
        store_strip(par, NEAR, values)

    def strips(step):
        par = step % 2
        source = dirs_at(step)
        for b in PLANS[phase][step][2]:
            slot, held, first, _ = BLOCKS[b]
            at = slice(b * LANES, (b + 1) * LANES)
            before, after = sdon[b, 0], sdon[b, 1]
            rows, far, mid = [[], [], [], []], [], []
            for h in range(2):
                d = sdirs[par, b, h]
                edge = jnp.zeros((8, LANES), jnp.float32)
                for c in range(held):
                    col = first + c
                    tile = source[slot + c, h, :, pl.ds(pl.multiple_of((1 - nrm) * LANES, LANES), LANES)]
                    tile = pltpu.roll(tile, HALO * col + 1 + 14 * nrm, 1)
                    edge = jnp.where((lane >= HALO * col) & (lane < HALO * (col + 1)), tile, edge)
                west, west2 = pltpu.roll(d, HALO, 1), pltpu.roll(d, 2 * HALO, 1)
                east, east2 = pltpu.roll(d, LANES - HALO, 1), pltpu.roll(d, LANES - 2 * HALO, 1)
                if b > 1:
                    other = sdirs[par, b - 1, h]
                    close = jnp.take_along_axis(other, jnp.bitwise_and(before + 7 * HALO, LANES - 1), axis=1)
                    next2 = jnp.take_along_axis(other, jnp.bitwise_and(before + 6 * HALO, LANES - 1), axis=1)
                    west = jnp.where(lane < HALO, close, west)
                    west2 = jnp.where(lane < 2 * HALO, next2, west2)
                if b < 3:
                    other = sdirs[par, b + 1, h]
                    close = jnp.take_along_axis(other, jnp.bitwise_and(after + HALO, LANES - 1), axis=1)
                    next2 = jnp.take_along_axis(other, jnp.bitwise_and(after + 2 * HALO, LANES - 1), axis=1)
                    east = jnp.where(lane >= 7 * HALO, close, east)
                    east2 = jnp.where(lane >= 6 * HALO, next2, east2)
                south = jnp.where(group == 0, edge, pltpu.roll(d, 1, 1))
                north = jnp.where(group == HALO - 1, edge, pltpu.roll(d, LANES - 1, 1))
                for face, value in enumerate((west, east, south, north)):
                    rows[face].append(spre[b, 2 + face : 3 + face] * value)
                far.append(west2 + east2)
                mid.append(d)
            high, low = split(jnp.concatenate(sum(rows, []), 0))
            out = apply(
                basis, jnp.concatenate([high, low, high], 0), mid, far, halo[SHIFT : SHIFT + 1, at], halo[DAMP : DAMP + 1, at],
                lambda m, at=at: halo[FLOW + m : FLOW + m + 1, at],
            )
            new = [sres[b, h] - out[h] for h in range(2)]
            keep, gain = steps[step]
            turned = precond(spre[b, 0:1], spre[b, 1:2], *new)
            made = [keep * mid[h] + gain * turned[h] for h in range(2)]
            if phase == LATE and b == OWN and step == MIDDLE:
                done = lane < EARLY_LANES
                new = [jnp.where(done, kept_res[h], new[h]) for h in range(2)]
                made = [jnp.where(done, kept_dirs[1, h], made[h]) for h in range(2)]
            for h in range(2):
                sres[b, h] = new[h]
                if phase == EARLY and step == MIDDLE:
                    kept_dirs[b - 1, h] = made[h]
                    if b == OWN:
                        kept_res[h] = new[h]
            store_strip(1 - par, b, made)

    def column(step, b, c):
        slot, _, first, _ = BLOCKS[b]
        s, q = slot + c, FIRST[b] + c
        par = step % 2
        p = parts_at(step)
        turn = 127 - 14 * nrm - HALO * (first + c)
        stack = [[], []]
        for k in range(2):
            tiles = [p[s, k, :, t * LANES : (t + 1) * LANES] for t in range(2)]
            up = [pltpu.roll(x, 1, 1) for x in tiles]
            down = [pltpu.roll(x, LANES - 1, 1) for x in tiles]
            south = [up[0], jnp.where(lane16 == 0, up[0], up[1])]
            north = [jnp.where(lane16 == LANES - 1, down[1], down[0]), down[1]]
            if phase != FIRST_HALF:
                edge = pltpu.roll(sparts[par, b, k], turn, 1)
                south[0] = jnp.where(lane16 == 0, edge, south[0])
                north[1] = jnp.where(lane16 == LANES - 1, edge, north[1])
            for face, value in enumerate(
                (p[s - 1, k], p[s + 1, k], jnp.concatenate(south, 1), jnp.concatenate(north, 1))
            ):
                stack[k].append(masks[q, face] * value)
        return jnp.concatenate(stack[0] + stack[1] + stack[0], 0)

    def write(c, total, left):
        i = place(OWN, c, odd)
        for h in range(2):
            sol_out[5 * h : 5 * h + 5, i, :] = total[h][0:5]
            res_out[5 * h : 5 * h + 5, i, :] = left[h][0:5]

    def finish(step, b, c, rows):
        s, q = BLOCKS[b][0] + c, FIRST[b] + c
        d = dirs_at(step)
        mid = [d[s, h] for h in range(2)]
        far = [d[s - 2, h] + d[s + 2, h] for h in range(2)]
        out = apply(basis, rows, mid, far, coef[q, 0:1], coef[q, 1:2], lambda m: coef[q, 8 + m : 9 + m])
        old = res0 if step == 0 else res
        new = [old[q, h] - out[h] for h in range(2)]
        for h in range(2):
            res[q, h] = new[h]
            if b == OWN:
                sol[c, h] = mid[h] if step == 0 else sol[c, h] + mid[h]
        if phase == LATE and step + 1 == ITERS:
            write(c, [sol[c, h] for h in range(2)], new)
        if step + 1 < ITERS:
            keep, gain = steps[step]
            turned = precond(coef[q, 2:3], coef[q, 3:4], *new)
            store(1 - step % 2, s, [keep * mid[h] + gain * turned[h] for h in range(2)])

    if phase == LATE:
        for c in range(2):
            write(c, [sol[c, h] for h in range(2)], [res[FIRST[OWN] + c, h] for h in range(2)])
    for step, (columns, fills, _) in PLANS[phase].items():
        par = step % 2
        for n in fills:
            ghosts(dirs.at[par], dirs.at[par], parts.at[par], index, n)
        strips(step)
        for b, start, pairs in columns:
            for c in range(start, start + 2 * pairs):
                finish(step, b, c, column(step, b, c))


def moved(cells, pairs):
    return lax.ppermute(cells, "blk", [p for p in pairs(lax.axis_size("blk"))])


def far_pairs(by):
    def pairs(count):
        for i in range(count):
            j = i - by if i % 2 == 0 else i + by
            if 0 <= j < count:
                yield j, i

    return pairs


def chip_pairs(count):
    return [(i, i + 1 - 2 * (i % 2)) for i in range(count)]


def local(kernel, outs, scratch, *args, limit=16 << 20, aliases=None):
    vmem = pl.BlockSpec(memory_space=pltpu.VMEM)
    return pl.pallas_call(
        kernel,
        out_shape=outs,
        in_specs=[vmem] * len(args),
        out_specs=jax.tree.map(lambda _: vmem, outs),
        scratch_shapes=scratch,
        input_output_aliases=aliases or {},
        compiler_params=pltpu.CompilerParams(vmem_limit_bytes=limit),
    )(*args)


def inside(x):
    return pltpu.with_memory_space_constraint(x, pltpu.VMEM)


def step(right_side, mean_flow, jac_basis, pattern, shift_diag, dissipation, donors):
    f32, bf16 = jnp.float32, jnp.bfloat16
    vmem = pltpu.VMEM

    whole, part = local(
        pack_kernel,
        (vmem((WHOLE_ROWS, LANES), f32), vmem((PART_ROWS, LANES), f32)),
        [],
        right_side, mean_flow, pattern, shift_diag, dissipation, donors,
        limit=None,
    )
    far1 = moved(whole, far_pairs(1))
    far2 = moved(part, far_pairs(2))
    near = moved(whole, chip_pairs)
    basis = local(
        basis_kernel, vmem((80, 192), bf16), [vmem((80, LANES), f32)], jac_basis.transpose(1, 2, 0, 3)
    )

    cells = [inside(x) for x in (far2, far1, whole, near)]
    strip = local(
        functools.partial(strip_kernel, (FAR2, OWN, NEAR)), vmem((FEATS, 4 * LANES), f32), [],
        *(cells[b] for b in (FAR2, OWN, NEAR)),
    )
    strip = local(
        functools.partial(strip_kernel, (FAR1,)), vmem((FEATS, 4 * LANES), f32), [], inside(strip), cells[FAR1]
    )
    halo = lax.ppermute(strip, "nrm", [(0, 1), (1, 0)])
    coef, masks, res0, dirs0, parts0, index = local(
        prep_kernel,
        (
            vmem((COLUMNS, 16, WIDTH), f32),
            vmem((COLUMNS, 4, 16, WIDTH), bf16),
            vmem((COLUMNS, 2, 8, WIDTH), f32),
            vmem((SLOTS, 2, 8, WIDTH), f32),
            vmem((SLOTS, 2, 16, WIDTH), bf16),
            vmem((6, 2, 8, LANES), jnp.int32),
        ),
        [],
        *cells,
    )

    basis = inside(basis)
    fixed = [inside(x) for x in (coef, masks)]
    index = inside(index)
    state = (
        vmem((2, SLOTS, 2, 8, WIDTH), f32),
        vmem((COLUMNS, 2, 8, WIDTH), f32),
        vmem((8, 2, 8, WIDTH), f32),
    )
    parts = vmem((2, SLOTS, 2, 16, WIDTH), bf16)
    dirs, res, sol = local(
        functools.partial(solve_kernel, FIRST_HALF), state, (parts,),
        *fixed, *[inside(x) for x in (res0, dirs0, parts0)], index, basis,
    )
    dirs, res, halo = inside(dirs), inside(res), inside(halo)
    *edges, message = local(
        edge_kernel,
        (
            vmem((4, 2, 8, LANES), f32),
            vmem((4, 2, 8, LANES), f32),
            vmem((2, 2, 8, LANES), f32),
            vmem((2, 2, 8, LANES), f32),
            vmem((2, 2, 8, LANES), f32),
            vmem((16 * (SENT_DIRS + SENT_RES + 1), WIDTH), f32),
        ),
        (
            vmem((7, FEATS, LANES), f32),
            vmem((7, 8, LANES), f32),
            vmem((7, 2, 8, LANES), jnp.int32),
            vmem((2, 7, 2, 8, LANES), f32),
            vmem((7, 2, 8, LANES), f32),
        ),
        inside(strip), halo, basis, dirs, res,
    )
    message = moved(message, chip_pairs)
    scratch = (
        vmem((2, 4, 2, 8, LANES), f32),
        vmem((4, 2, 8, LANES), f32),
        vmem((2, 4, 2, 16, LANES), bf16),
        vmem((4, 8, LANES), f32),
        vmem((4, 2, 8, LANES), jnp.int32),
    )
    edges = [inside(x) for x in edges]
    kept = local(
        functools.partial(solve_kernel, EARLY),
        (*state, parts, vmem((2, 2, 8, LANES), f32), vmem((2, 8, LANES), f32)),
        scratch,
        *fixed, dirs, res, inside(sol), *edges, index, halo, basis,
    )
    out = jax.ShapeDtypeStruct(right_side.shape, f32)
    return local(
        functools.partial(solve_kernel, LATE), (out, out, *state, parts), scratch,
        *fixed, *[inside(x) for x in kept], *edges[3:], inside(message), index, halo, basis,
        aliases={2: 2, 3: 3, 4: 4, 5: 5},
    )[:2]


def solution(mesh):
    return jax.shard_map(
        step,
        mesh=mesh,
        in_specs=(
            P(None, "blk", "nrm"),
            P(None, "blk", "nrm"),
            P(),
            P(None, "blk", "nrm"),
            P("blk", "nrm"),
            P("blk", "nrm"),
            P("blk", None, "nrm"),
        ),
        out_specs=(P(None, "blk", "nrm"), P(None, "blk", "nrm")),
        check_vma=False,
    )
```

```python
import functools

import jax
import jax.numpy as jnp
from jax import lax
from jax.experimental import pallas as pl
from jax.experimental.pallas import tpu as pltpu
from jax.sharding import PartitionSpec as P


ITERS = 6
OMEGA = 0.3
DELTA = 0.9

SHIFT, DAMP, DON0, DON1 = 5, 6, 21, 22
MASK = (7, 13, 14, 15)
FLOW = 16
WHOLE_B, WHOLE_FLOW, WHOLE_DON, WHOLE_ROWS = 128, 256, 336, 344
PART_B, PART_FLOW, PART_DON, PART_ROWS = 64, 128, 148, 152
FEATS = 24
HALO = 16
LANES = 128
WIDTH = 256

FAR2, FAR1, OWN, NEAR = 0, 1, 2, 3
BLOCKS = ((0, 4, 4, 4), (8, 8, 0, 8), (20, 8, 0, 8), (32, 6, 0, 8))
FIRST = (0, 4, 12, 20)
COLUMNS = 26
SLOTS = 38
MIDDLE = 3
FIRST_HALF, EARLY, LATE = 0, 1, 2
PLANS = (
    {
        0: (((0, 2, 1), (1, 0, 4), (2, 0, 4), (3, 0, 2)), (), ()),
        1: (((1, 0, 4), (2, 0, 4), (3, 0, 1)), (1, 2, 3, 4, 5), ()),
        2: (((1, 2, 3), (2, 0, 4)), (2, 3, 4), ()),
    },
    {
        3: (((1, 4, 2), (2, 0, 3)), (2, 3), (1, 2)),
        4: (((1, 6, 1), (2, 0, 2)), (2, 3), (2,)),
        5: (((2, 0, 1),), (3,), ()),
    },
    {
        3: (((2, 6, 1), (3, 0, 2)), (4, 5), (2, 3)),
        4: (((2, 4, 2), (3, 0, 1)), (4, 5), (2,)),
        5: (((2, 2, 3),), (4,), ()),
    },
)
EARLY_LANES = 6 * HALO
TILES = ((0, 1), (1, 0), (1, 1), (2, 0), (2, 1), (3, 0), (3, 1))
TILES_AT = (range(0, 6), range(1, 6), range(1, 5))
FIX = 1 + 3 * (MIDDLE - 1)
LISTS = ((0, 1), (1, 0), (1, 1), (2, 0), (2, 1), (3, 0))
FILLS = ((4, 8, 0), (6, 2, 1), (16, 20, 2), (18, 14, 3), (28, 32, 4), (30, 26, 5))
SENT_DIRS, SENT_RES = 6, 4


def chebyshev():
    sigma = 1.0 / DELTA
    rho = DELTA
    steps = []
    for _ in range(ITERS - 1):
        rho_new = 1.0 / (2.0 * sigma - rho)
        steps.append((rho_new * rho, 2.0 * rho_new / DELTA))
        rho = rho_new
    return steps


def split(full):
    high = full.astype(jnp.bfloat16)
    return high, (full - high.astype(jnp.float32)).astype(jnp.bfloat16)


def precond(pa, pb, a, b):
    return pa * a + pb * b, pa * b - pb * a


def lanes(rows):
    return lax.broadcasted_iota(jnp.int32, (rows, LANES), 1)


def mirrored():
    return lax.rem(lax.axis_index("blk"), 2)


def place(b, c, odd):
    return c if b == FAR2 else c + odd * (7 - 2 * c)


def flow_row(b, c, m, t, odd):
    if b == FAR2:
        return PART_FLOW + 10 * (c - 2) + 2 * m + t if c >= 2 else None
    return WHOLE_FLOW + 8 * (2 * m + t) + place(b, c, odd)


def donor_row(b, side, t, odd):
    if b == FAR2:
        return PART_DON + t
    return WHOLE_DON + 2 * (side + odd * (1 - 2 * side)) + t


def pack_kernel(rhs, flow, mask, shift, damp, donors, whole, part):
    nrm, odd = lax.axis_index("nrm"), mirrored()
    count, width = rhs.shape[1:]
    here = lax.broadcasted_iota(jnp.int32, (1, width), 1) + nrm * width
    offsets = (donors[0] - here).astype(jnp.float32)
    for t in range(2):
        half = slice(t * LANES, (t + 1) * LANES)
        for i in range(count):
            at = 8 * (2 * i + t)
            whole[at : at + 5] = rhs[0:5, i, half]
            whole[at + SHIFT : at + SHIFT + 1] = shift[i : i + 1, half]
            whole[at + DAMP : at + DAMP + 1] = damp[i : i + 1, half]
            whole[at + 7 : at + 8] = mask[0:1, i, half].astype(jnp.float32)
            at = at + WHOLE_B
            whole[at : at + 5] = rhs[5:10, i, half]
            whole[at + 5 : at + 8] = mask[1:4, i, half].astype(jnp.float32)
        for m in range(5):
            at = WHOLE_FLOW + 8 * (2 * m + t)
            whole[at : at + 8] = flow[m, :, half]
        for side in range(2):
            at = WHOLE_DON + 2 * side + t
            whole[at : at + 1] = offsets[side : side + 1, half]
    whole[WHOLE_DON + 4 : WHOLE_ROWS] = jnp.zeros((4, LANES), jnp.float32)
    for c in range(4):
        p = place(OWN, 4 + c, odd)
        for t in range(2):
            for to, base in ((0, 0), (PART_B, WHOLE_B)):
                at = pl.multiple_of(base + 8 * (2 * p + t), 8)
                part[to + 8 * (2 * c + t) : to + 8 * (2 * c + t) + 8] = whole[pl.ds(at, 8)]
            for m in range(5):
                to = flow_row(FAR2, c, m, t, odd)
                if to is not None:
                    part[to : to + 1] = whole[pl.ds(flow_row(OWN, 4 + c, m, t, odd), 1)]
    for t in range(2):
        part[PART_DON + t : PART_DON + t + 1] = whole[pl.ds(donor_row(OWN, 1, t, odd), 1)]
    part[PART_DON + 2 : PART_ROWS] = jnp.zeros((2, LANES), jnp.float32)


def basis_kernel(jac, basis, full):
    full[...] = jnp.zeros(full.shape, jnp.float32)
    for f in range(4):
        for m in range(5):
            for h in range(2):
                for g in range(2):
                    block = jac[m, 5 * h : 5 * h + 5, f, 5 * g : 5 * g + 5]
                    full[16 * m + 8 * h : 16 * m + 8 * h + 5, 16 * f + 8 * g : 16 * f + 8 * g + 5] = block
    j = full[...]
    lane = lanes(80)
    other = jnp.where(lane < 16, pltpu.roll(j, LANES - 16, 1), pltpu.roll(j, 16, 1))
    j = jnp.where((mirrored() == 1) & (lane < 32), other, j)[:, 0:64]
    high, low = split(j)
    basis[:, 0:64] = high
    basis[:, 64:128] = high
    basis[:, 128:192] = low


def strip_kernel(blocks, *refs):
    nrm, odd = lax.axis_index("nrm"), mirrored()
    strip = refs[-1]
    lane = lanes(FEATS)
    t = 1 - nrm
    if len(blocks) == 1:
        strip[...] = refs[0][...]
    for b, ref in zip(blocks, refs[-1 - len(blocks) : -1], strict=True):
        first, sent = BLOCKS[b][2:]
        second = PART_B if b == FAR2 else WHOLE_B
        rows = jnp.zeros((FEATS, LANES), jnp.float32)
        lists = [ref[pl.ds(donor_row(b, side, t, 0), 1)] for side in range(2)]
        for c in range(sent):
            at = 8 * (2 * place(b, c, odd) + t)
            col = first + c
            edge = [ref[pl.ds(pl.multiple_of(base + at, 8), 8)] for base in (0, second)]
            if flow_row(b, c, 0, 0, 0) is None:
                edge.append(jnp.zeros((8, LANES), jnp.float32))
            else:
                flows = [ref[pl.ds(flow_row(b, c, m, t, odd), 1)] for m in range(5)]
                edge.append(jnp.concatenate(flows + lists + [jnp.zeros((1, LANES), jnp.float32)], 0))
            edge = pltpu.roll(jnp.concatenate(edge, 0), lax.rem(HALO * (col + 1 - nrm), LANES), 1)
            rows = jnp.where((lane >= HALO * col) & (lane < HALO * (col + 1)), edge, rows)
        strip[:, b * LANES : (b + 1) * LANES] = rows


def ghosts(src_d, dst_d, dst_h, index, n):
    dst, src, which = FILLS[n]
    lane = lanes(8)
    for c in range(2):
        for t in range(2):
            at = index[which, t]
            across = jnp.abs(at - lane) > LANES // 2
            picked = []
            for h in range(2):
                tiles = [src_d[src + c, h, :, u * LANES : (u + 1) * LANES] for u in (t, 1 - t)]
                here, there = (jnp.take_along_axis(x, at, axis=1) for x in tiles)
                picked.append(jnp.where(across, there, here))
                dst_d[dst + c, h, :, t * LANES : (t + 1) * LANES] = picked[h]
            high, low = split(jnp.concatenate(picked, 0))
            dst_h[dst + c, 0, :, t * LANES : (t + 1) * LANES] = high
            dst_h[dst + c, 1, :, t * LANES : (t + 1) * LANES] = low


def prep_kernel(far2, far1, own, near, coef, masks, res, dirs, parts, index):
    nrm, odd = lax.axis_index("nrm"), mirrored()
    refs = (far2, far1, own, near)
    row = lax.broadcasted_iota(jnp.int32, (8, WIDTH), 0)
    lane = lax.broadcasted_iota(jnp.int32, (16, WIDTH), 1)
    wall = ((lane == 0) & (nrm == 0), (lane == WIDTH - 1) & (nrm == 1))
    for b, ref in enumerate(refs):
        slot, held = BLOCKS[b][:2]
        second = PART_B if b == FAR2 else WHOLE_B
        for c in range(held):
            q, s = FIRST[b] + c, slot + c
            at = 16 * place(b, c, odd)

            def both(row, count, ref=ref, at=at, second=second):
                base = at + (row if row < 8 else second + row - 8)
                if count == 8:
                    base = pl.multiple_of(base, 8)
                return jnp.concatenate([ref[pl.ds(base, count)], ref[pl.ds(base + 8, count)]], 1)

            shift = both(SHIFT, 1)
            scale = 1.0 / (shift * shift + OMEGA * OMEGA)
            pa, pb = shift * scale, OMEGA * scale
            coef[q, 0:1] = shift
            coef[q, 1:2] = both(DAMP, 1)
            coef[q, 2:3] = pa
            coef[q, 3:4] = pb
            for m in range(5):
                for t in range(2):
                    r = flow_row(b, c, m, t, odd)
                    if r is not None:
                        coef[q, 8 + m : 9 + m, t * LANES : (t + 1) * LANES] = ref[pl.ds(r, 1)]
            m = [both(MASK[face], 1) for face in range(4)]
            m[0], m[1] = jnp.where(odd == 1, m[1], m[0]), jnp.where(odd == 1, m[0], m[1])
            for face in range(4):
                wide = jnp.broadcast_to(m[face], (16, WIDTH))
                if face >= 2:
                    wide = jnp.where(wall[face - 2], 0.0, wide)
                masks[q, face] = wide.astype(jnp.bfloat16)
            x = jnp.where(row < 5, both(0, 8), 0.0)
            y = jnp.where(row < 5, both(8, 8), 0.0)
            res[q, 0] = x
            res[q, 1] = y
            dx, dy = precond(pa, pb, x, y)
            dirs[s, 0] = dx
            dirs[s, 1] = dy
            high, low = split(jnp.concatenate([dx, dy], 0))
            parts[s, 0] = high
            parts[s, 1] = low
    for n, (b, side) in enumerate(LISTS):
        for t in range(2):
            offset = refs[b][pl.ds(donor_row(b, side, t, odd), 1)].astype(jnp.int32)
            index[n, t] = jnp.bitwise_and(lanes(8) + offset, LANES - 1)
    for n in range(len(FILLS)):
        ghosts(dirs, dirs, parts, index, n)


def patched(main, tile, c, nrm):
    lane = lax.broadcasted_iota(jnp.int32, (8, WIDTH), 1)
    tile = pltpu.roll(tile, 7 * HALO - 2 * HALO * (c % 4), 1)
    return jnp.where(
        jnp.where(nrm == 0, WIDTH - 1 - lane, lane) < FIX, jnp.concatenate([tile, tile], 1), main
    )


def apply(basis, rows, d, far, shift, damp, flow):
    y = jnp.dot(basis[...], rows, preferred_element_type=jnp.float32)
    out = [shift * d[0] - OMEGA * d[1], shift * d[1] + OMEGA * d[0]]
    for h in range(2):
        out[h] = out[h] + damp * far[h]
    for m in range(5):
        f = flow(m)
        for h in range(2):
            out[h] = out[h] + f * y[16 * m + 8 * h : 16 * m + 8 * h + 8]
    return out


def edge_kernel(
    strip, halo, basis, dirs, res, ed, er, es, sdirs, sres, message, feat, pre, don, cur, rem,
):
    nrm, odd = lax.axis_index("nrm"), mirrored()
    lane = lanes(8)
    wide = lanes(FEATS)
    low_rows = lax.broadcasted_iota(jnp.int32, (8, LANES), 0) < 5
    steps = chebyshev()
    for e, (b, t) in enumerate(TILES):
        at = slice(b * LANES, (b + 1) * LANES)
        mine, theirs = strip[:, at], halo[:, at]
        pair = (jnp.where(nrm == 0, mine, theirs), jnp.where(nrm == 0, theirs, mine))
        from_lane = HALO * (4 * t + jnp.right_shift(lane, 5)) + jnp.bitwise_and(lane, HALO - 1)
        for k in range(3):
            picked = [jnp.take_along_axis(x[8 * k : 8 * k + 8], from_lane, axis=1) for x in pair]
            feat[e, 8 * k : 8 * k + 8] = jnp.where(jnp.bitwise_and(lane, HALO) == 0, *picked)
        shift = feat[e, SHIFT : SHIFT + 1]
        scale = 1.0 / (shift * shift + OMEGA * OMEGA)
        pre[e, 0:1] = shift * scale
        pre[e, 1:2] = OMEGA * scale
        m = [feat[e, MASK[face] : MASK[face] + 1] for face in range(4)]
        pre[e, 2:3] = jnp.where(odd == 1, m[1], m[0])
        pre[e, 3:4] = jnp.where(odd == 1, m[0], m[1])
        pre[e, 4:5] = m[2]
        pre[e, 5:6] = m[3]
        pair = [feat[e, r : r + 1] for r in (DON0, DON1)]
        don[e, 0] = jnp.where(odd == 1, pair[1], pair[0]).astype(jnp.int32) + lane
        don[e, 1] = jnp.where(odd == 1, pair[0], pair[1]).astype(jnp.int32) + lane
        x = [jnp.where(low_rows, feat[e, 8 * h : 8 * h + 8], 0.0) for h in range(2)]
        made = precond(shift * scale, OMEGA * scale, *x)
        for h in range(2):
            rem[e, h] = x[h]
            cur[0, e, h] = made[h]

    span = 2 * HALO
    for step in range(MIDDLE):
        par = step % 2
        for e in TILES_AT[step]:
            b, t = TILES[e]
            rows, far, mid = [[], [], [], []], [], []
            for h in range(2):
                d = cur[par, e, h]
                west, west2 = pltpu.roll(d, span, 1), pltpu.roll(d, 2 * span, 1)
                east, east2 = pltpu.roll(d, LANES - span, 1), pltpu.roll(d, LANES - 2 * span, 1)
                if e > 0:
                    other = cur[par, e - 1, h]
                    if t == 0:
                        close = jnp.take_along_axis(other, jnp.bitwise_and(don[e, 0] + 3 * span, LANES - 1), axis=1)
                        next2 = jnp.take_along_axis(other, jnp.bitwise_and(don[e, 0] + 2 * span, LANES - 1), axis=1)
                    else:
                        close, next2 = pltpu.roll(other, span, 1), pltpu.roll(other, 2 * span, 1)
                    west = jnp.where(lane < span, close, west)
                    west2 = jnp.where(lane < 2 * span, next2, west2)
                if e + 1 < len(TILES):
                    other = cur[par, e + 1, h]
                    if t == 1:
                        close = jnp.take_along_axis(other, jnp.bitwise_and(don[e, 1] + span, LANES - 1), axis=1)
                        next2 = jnp.take_along_axis(other, jnp.bitwise_and(don[e, 1] + 2 * span, LANES - 1), axis=1)
                    else:
                        close, next2 = pltpu.roll(other, LANES - span, 1), pltpu.roll(other, LANES - 2 * span, 1)
                    east = jnp.where(lane >= 3 * span, close, east)
                    east2 = jnp.where(lane >= 2 * span, next2, east2)
                for face, value in enumerate((west, east, pltpu.roll(d, 1, 1), pltpu.roll(d, LANES - 1, 1))):
                    rows[face].append(pre[e, 2 + face : 3 + face] * value)
                far.append(west2 + east2)
                mid.append(d)
            high, low = split(jnp.concatenate(sum(rows, []), 0))
            out = apply(
                basis, jnp.concatenate([high, low, high], 0), mid, far,
                feat[e, SHIFT : SHIFT + 1], feat[e, DAMP : DAMP + 1], lambda m, e=e: feat[e, FLOW + m : FLOW + m + 1],
            )
            new = [rem[e, h] - out[h] for h in range(2)]
            keep, gain = steps[step]
            turned = precond(pre[e, 0:1], pre[e, 1:2], *new)
            for h in range(2):
                rem[e, h] = new[h]
                cur[1 - par, e, h] = keep * mid[h] + gain * turned[h]
                if b == OWN:
                    es[t, h] = mid[h] if step == 0 else es[t, h] + mid[h]

    par = MIDDLE % 2
    from_lane = span * jnp.bitwise_and(jnp.right_shift(lane, 4), 3) + HALO * (1 - nrm) + jnp.bitwise_and(lane, HALO - 1)
    for e in range(1, 5):
        for h in range(2):
            ed[e - 1, h] = cur[par, e, h]
            er[e - 1, h] = rem[e, h]
    for b in (FAR1, OWN):
        for h in range(2):
            for out, tiles in ((sdirs, cur.at[par]), (sres, rem)):
                halves = [jnp.take_along_axis(tiles[2 * b - 1 + t, h], from_lane, axis=1) for t in range(2)]
                out[b - 1, h] = jnp.where(lane < LANES // 2, *halves)

    for n in range(SENT_DIRS):
        c = 7 - n
        for h in range(2):
            at = 8 * (2 * n + h)
            message[at : at + 8, :] = patched(dirs[par, BLOCKS[OWN][0] + c, h], ed[2 + c // 4, h], c, nrm)
    for n in range(SENT_RES):
        c = 7 - n
        for h in range(2):
            at = 16 * SENT_DIRS + 8 * (2 * n + h)
            message[at : at + 8, :] = patched(res[FIRST[OWN] + c, h], er[2 + c // 4, h], c, nrm)
    at = 16 * (SENT_DIRS + SENT_RES)
    for h in range(2):
        message[at + 8 * h : at + 8 * h + 8, 0:LANES] = sdirs[OWN - 1, h]
        message[at + 8 * h : at + 8 * h + 8, LANES:] = sres[OWN - 1, h]


def solve_kernel(phase, *refs):
    if phase == FIRST_HALF:
        (coef, masks, res0, dirs0, parts0, index, basis) = refs[:7]
        (dirs, res, sol, parts) = refs[7:]
    elif phase == EARLY:
        (coef, masks, _, _, _, _, ed, er, es, old_sdirs, old_sres, index, halo, basis) = refs[:14]
        (dirs, res, sol, parts, kept_dirs, kept_res, sdirs, sres, sparts, spre, sdon) = refs[14:]
    else:
        (coef, masks, _, _, _, _, kept_dirs, kept_res, old_sdirs, old_sres, message, index, halo, basis) = refs[:14]
        (sol_out, res_out, dirs, res, sol, parts, sdirs, sres, sparts, spre, sdon) = refs[14:]
    nrm, odd = lax.axis_index("nrm"), mirrored()
    lane = lanes(8)
    lane16 = lanes(16)
    group = jnp.bitwise_and(lane, HALO - 1)
    low_rows = lax.broadcasted_iota(jnp.int32, (8, LANES), 0) < 5
    steps = chebyshev()

    def dirs_at(step):
        return dirs0 if step == 0 else dirs.at[step % 2]

    def parts_at(step):
        return parts0 if step == 0 else parts.at[step % 2]

    def store(par, s, values):
        for h in range(2):
            dirs[par, s, h] = values[h]
        high, low = split(jnp.concatenate(values, 0))
        parts[par, s, 0] = high
        parts[par, s, 1] = low

    def store_strip(par, b, values):
        for h in range(2):
            sdirs[par, b, h] = values[h]
        high, low = split(jnp.concatenate(values, 0))
        sparts[par, b, 0] = high
        sparts[par, b, 1] = low

    if phase != FIRST_HALF:
        for b in (FAR1, OWN) if phase == EARLY else (OWN, NEAR):
            at = slice(b * LANES, (b + 1) * LANES)
            shift = halo[SHIFT : SHIFT + 1, at]
            scale = 1.0 / (shift * shift + OMEGA * OMEGA)
            spre[b, 0:1] = shift * scale
            spre[b, 1:2] = OMEGA * scale
            m = [halo[MASK[face] : MASK[face] + 1, at] for face in range(4)]
            spre[b, 2:3] = jnp.where(odd == 1, m[1], m[0])
            spre[b, 3:4] = jnp.where(odd == 1, m[0], m[1])
            spre[b, 4:5] = m[2]
            spre[b, 5:6] = m[3]
            pair = [halo[r : r + 1, at] for r in (DON0, DON1)]
            sdon[b, 0] = jnp.where(odd == 1, pair[1], pair[0]).astype(jnp.int32) + lane
            sdon[b, 1] = jnp.where(odd == 1, pair[0], pair[1]).astype(jnp.int32) + lane
        par = MIDDLE % 2
        for b in (FAR1, OWN):
            store_strip(par, b, [old_sdirs[b - 1, h] for h in range(2)])
            for h in range(2):
                sres[b, h] = old_sres[b - 1, h]
    if phase == EARLY:
        blank = [jnp.zeros((8, LANES), jnp.float32)] * 2
        store_strip(0, NEAR, blank)
        store_strip(1, NEAR, blank)
        at = pl.ds(pl.multiple_of((1 - nrm) * LANES, LANES), LANES)
        close = jnp.where(nrm == 0, LANES - 1 - lane, lane) < FIX

        def mend(ref, tile, c):
            value = jnp.where(close, pltpu.roll(tile, 7 * HALO - 2 * HALO * (c % 4), 1), ref[:, at])
            ref[:, at] = value
            return value

        for b, kept in ((FAR1, range(2, 8)), (OWN, range(8))):
            for c in kept:
                s, q, e = BLOCKS[b][0] + c, FIRST[b] + c, 2 * (b - 1) + c // 4
                high, low = split(jnp.concatenate([mend(dirs.at[par, s, h], ed[e, h], c) for h in range(2)], 0))
                parts[par, s, 0, :, at] = high
                parts[par, s, 1, :, at] = low
                for h in range(2):
                    mend(res.at[q, h], er[e, h], c)
                    if b == OWN:
                        mend(sol.at[c, h], es[c // 4, h], c)
    if phase == LATE:
        store_strip(1 - par, FAR1, [kept_dirs[0, h] for h in range(2)])
        slot, first = BLOCKS[NEAR][0], FIRST[NEAR]
        for n in range(SENT_DIRS):
            at = 16 * n
            store(par, slot + n, [message[at + 8 * h : at + 8 * h + 8, :] for h in range(2)])
        for n in range(SENT_RES):
            for h in range(2):
                at = 16 * (SENT_DIRS + n) + 8 * h
                res[first + n, h] = message[at : at + 8, :]
        swap = 7 * HALO - (lane - group) + group
        at = 16 * (SENT_DIRS + SENT_RES)
        values = []
        for h in range(2):
            rows = slice(at + 8 * h, at + 8 * h + 8)
            values.append(jnp.take_along_axis(message[rows, 0:LANES], swap, axis=1))
            sres[NEAR, h] = jnp.take_along_axis(message[rows, LANES:], swap, axis=1)
        store_strip(par, NEAR, values)

    def strips(step):
        par = step % 2
        source = dirs_at(step)
        for b in PLANS[phase][step][2]:
            slot, held, first, _ = BLOCKS[b]
            at = slice(b * LANES, (b + 1) * LANES)
            before, after = sdon[b, 0], sdon[b, 1]
            rows, far, mid = [[], [], [], []], [], []
            for h in range(2):
                d = sdirs[par, b, h]
                edge = jnp.zeros((8, LANES), jnp.float32)
                for c in range(held):
                    col = first + c
                    tile = source[slot + c, h, :, pl.ds(pl.multiple_of((1 - nrm) * LANES, LANES), LANES)]
                    tile = pltpu.roll(tile, HALO * col + 1 + 14 * nrm, 1)
                    edge = jnp.where((lane >= HALO * col) & (lane < HALO * (col + 1)), tile, edge)
                west, west2 = pltpu.roll(d, HALO, 1), pltpu.roll(d, 2 * HALO, 1)
                east, east2 = pltpu.roll(d, LANES - HALO, 1), pltpu.roll(d, LANES - 2 * HALO, 1)
                if b > 1:
                    other = sdirs[par, b - 1, h]
                    close = jnp.take_along_axis(other, jnp.bitwise_and(before + 7 * HALO, LANES - 1), axis=1)
                    next2 = jnp.take_along_axis(other, jnp.bitwise_and(before + 6 * HALO, LANES - 1), axis=1)
                    west = jnp.where(lane < HALO, close, west)
                    west2 = jnp.where(lane < 2 * HALO, next2, west2)
                if b < 3:
                    other = sdirs[par, b + 1, h]
                    close = jnp.take_along_axis(other, jnp.bitwise_and(after + HALO, LANES - 1), axis=1)
                    next2 = jnp.take_along_axis(other, jnp.bitwise_and(after + 2 * HALO, LANES - 1), axis=1)
                    east = jnp.where(lane >= 7 * HALO, close, east)
                    east2 = jnp.where(lane >= 6 * HALO, next2, east2)
                south = jnp.where(group == 0, edge, pltpu.roll(d, 1, 1))
                north = jnp.where(group == HALO - 1, edge, pltpu.roll(d, LANES - 1, 1))
                for face, value in enumerate((west, east, south, north)):
                    rows[face].append(spre[b, 2 + face : 3 + face] * value)
                far.append(west2 + east2)
                mid.append(d)
            high, low = split(jnp.concatenate(sum(rows, []), 0))
            out = apply(
                basis, jnp.concatenate([high, low, high], 0), mid, far, halo[SHIFT : SHIFT + 1, at], halo[DAMP : DAMP + 1, at],
                lambda m, at=at: halo[FLOW + m : FLOW + m + 1, at],
            )
            new = [sres[b, h] - out[h] for h in range(2)]
            keep, gain = steps[step]
            turned = precond(spre[b, 0:1], spre[b, 1:2], *new)
            made = [keep * mid[h] + gain * turned[h] for h in range(2)]
            if phase == LATE and b == OWN and step == MIDDLE:
                done = lane < EARLY_LANES
                new = [jnp.where(done, kept_res[h], new[h]) for h in range(2)]
                made = [jnp.where(done, kept_dirs[1, h], made[h]) for h in range(2)]
            for h in range(2):
                sres[b, h] = new[h]
                if phase == EARLY and step == MIDDLE:
                    kept_dirs[b - 1, h] = made[h]
                    if b == OWN:
                        kept_res[h] = new[h]
            store_strip(1 - par, b, made)

    def column(step, b, c):
        slot, _, first, _ = BLOCKS[b]
        s, q = slot + c, FIRST[b] + c
        par = step % 2
        p = parts_at(step)
        turn = 127 - 14 * nrm - HALO * (first + c)
        stack = [[], []]
        for k in range(2):
            tiles = [p[s, k, :, t * LANES : (t + 1) * LANES] for t in range(2)]
            up = [pltpu.roll(x, 1, 1) for x in tiles]
            down = [pltpu.roll(x, LANES - 1, 1) for x in tiles]
            south = [up[0], jnp.where(lane16 == 0, up[0], up[1])]
            north = [jnp.where(lane16 == LANES - 1, down[1], down[0]), down[1]]
            if phase != FIRST_HALF:
                edge = pltpu.roll(sparts[par, b, k], turn, 1)
                south[0] = jnp.where(lane16 == 0, edge, south[0])
                north[1] = jnp.where(lane16 == LANES - 1, edge, north[1])
            for face, value in enumerate(
                (p[s - 1, k], p[s + 1, k], jnp.concatenate(south, 1), jnp.concatenate(north, 1))
            ):
                stack[k].append(masks[q, face] * value)
        return jnp.concatenate(stack[0] + stack[1] + stack[0], 0)

    def write(c, total, left):
        i = place(OWN, c, odd)
        for h in range(2):
            sol_out[5 * h : 5 * h + 5, i, :] = total[h][0:5]
            res_out[5 * h : 5 * h + 5, i, :] = left[h][0:5]

    def finish(step, b, c, rows):
        s, q = BLOCKS[b][0] + c, FIRST[b] + c
        d = dirs_at(step)
        mid = [d[s, h] for h in range(2)]
        far = [d[s - 2, h] + d[s + 2, h] for h in range(2)]
        out = apply(basis, rows, mid, far, coef[q, 0:1], coef[q, 1:2], lambda m: coef[q, 8 + m : 9 + m])
        old = res0 if step == 0 else res
        new = [old[q, h] - out[h] for h in range(2)]
        for h in range(2):
            res[q, h] = new[h]
            if b == OWN:
                sol[c, h] = mid[h] if step == 0 else sol[c, h] + mid[h]
        if phase == LATE and step + 1 == ITERS:
            write(c, [sol[c, h] for h in range(2)], new)
        if step + 1 < ITERS:
            keep, gain = steps[step]
            turned = precond(coef[q, 2:3], coef[q, 3:4], *new)
            store(1 - step % 2, s, [keep * mid[h] + gain * turned[h] for h in range(2)])

    if phase == LATE:
        for c in range(2):
            write(c, [sol[c, h] for h in range(2)], [res[FIRST[OWN] + c, h] for h in range(2)])
    for step, (columns, fills, _) in PLANS[phase].items():
        par = step % 2
        for n in fills:
            ghosts(dirs.at[par], dirs.at[par], parts.at[par], index, n)
        strips(step)
        for b, start, pairs in columns:
            for c in range(start, start + 2 * pairs):
                finish(step, b, c, column(step, b, c))


def moved(cells, pairs):
    return lax.ppermute(cells, "blk", [p for p in pairs(lax.axis_size("blk"))])


def far_pairs(by):
    def pairs(count):
        for i in range(count):
            j = i - by if i % 2 == 0 else i + by
            if 0 <= j < count:
                yield j, i

    return pairs


def chip_pairs(count):
    return [(i, i + 1 - 2 * (i % 2)) for i in range(count)]


def local(kernel, outs, scratch, *args, limit=16 << 20, aliases=None):
    vmem = pl.BlockSpec(memory_space=pltpu.VMEM)
    return pl.pallas_call(
        kernel,
        out_shape=outs,
        in_specs=[vmem] * len(args),
        out_specs=jax.tree.map(lambda _: vmem, outs),
        scratch_shapes=scratch,
        input_output_aliases=aliases or {},
        compiler_params=pltpu.CompilerParams(vmem_limit_bytes=limit),
    )(*args)


def inside(x):
    return pltpu.with_memory_space_constraint(x, pltpu.VMEM)


def step(right_side, mean_flow, jac_basis, pattern, shift_diag, dissipation, donors):
    f32, bf16 = jnp.float32, jnp.bfloat16
    vmem = pltpu.VMEM

    whole, part = local(
        pack_kernel,
        (vmem((WHOLE_ROWS, LANES), f32), vmem((PART_ROWS, LANES), f32)),
        [],
        right_side, mean_flow, pattern, shift_diag, dissipation, donors,
        limit=None,
    )
    far1 = moved(whole, far_pairs(1))
    far2 = moved(part, far_pairs(2))
    near = moved(whole, chip_pairs)
    basis = local(
        basis_kernel, vmem((80, 192), bf16), [vmem((80, LANES), f32)], jac_basis.transpose(1, 2, 0, 3)
    )

    cells = [inside(x) for x in (far2, far1, whole, near)]
    strip = local(
        functools.partial(strip_kernel, (FAR2, OWN, NEAR)), vmem((FEATS, 4 * LANES), f32), [],
        *(cells[b] for b in (FAR2, OWN, NEAR)),
    )
    strip = local(
        functools.partial(strip_kernel, (FAR1,)), vmem((FEATS, 4 * LANES), f32), [], inside(strip), cells[FAR1]
    )
    halo = lax.ppermute(strip, "nrm", [(0, 1), (1, 0)])
    coef, masks, res0, dirs0, parts0, index = local(
        prep_kernel,
        (
            vmem((COLUMNS, 16, WIDTH), f32),
            vmem((COLUMNS, 4, 16, WIDTH), bf16),
            vmem((COLUMNS, 2, 8, WIDTH), f32),
            vmem((SLOTS, 2, 8, WIDTH), f32),
            vmem((SLOTS, 2, 16, WIDTH), bf16),
            vmem((6, 2, 8, LANES), jnp.int32),
        ),
        [],
        *cells,
    )

    basis = inside(basis)
    fixed = [inside(x) for x in (coef, masks)]
    index = inside(index)
    state = (
        vmem((2, SLOTS, 2, 8, WIDTH), f32),
        vmem((COLUMNS, 2, 8, WIDTH), f32),
        vmem((8, 2, 8, WIDTH), f32),
    )
    parts = vmem((2, SLOTS, 2, 16, WIDTH), bf16)
    dirs, res, sol, pieces = local(
        functools.partial(solve_kernel, FIRST_HALF), (*state, parts), (),
        *fixed, *[inside(x) for x in (res0, dirs0, parts0)], index, basis,
    )
    dirs, res, halo = inside(dirs), inside(res), inside(halo)
    *edges, message = local(
        edge_kernel,
        (
            vmem((4, 2, 8, LANES), f32),
            vmem((4, 2, 8, LANES), f32),
            vmem((2, 2, 8, LANES), f32),
            vmem((2, 2, 8, LANES), f32),
            vmem((2, 2, 8, LANES), f32),
            vmem((16 * (SENT_DIRS + SENT_RES + 1), WIDTH), f32),
        ),
        (
            vmem((7, FEATS, LANES), f32),
            vmem((7, 8, LANES), f32),
            vmem((7, 2, 8, LANES), jnp.int32),
            vmem((2, 7, 2, 8, LANES), f32),
            vmem((7, 2, 8, LANES), f32),
        ),
        inside(strip), halo, basis, dirs, res,
    )
    message = moved(message, chip_pairs)
    scratch = (
        vmem((2, 4, 2, 8, LANES), f32),
        vmem((4, 2, 8, LANES), f32),
        vmem((2, 4, 2, 16, LANES), bf16),
        vmem((4, 8, LANES), f32),
        vmem((4, 2, 8, LANES), jnp.int32),
    )
    edges = [inside(x) for x in edges]
    kept = local(
        functools.partial(solve_kernel, EARLY),
        (*state, parts, vmem((2, 2, 8, LANES), f32), vmem((2, 8, LANES), f32)),
        scratch,
        *fixed, dirs, res, inside(sol), inside(pieces), *edges, index, halo, basis,
        aliases={2: 0, 3: 1, 4: 2, 5: 3},
    )
    out = jax.ShapeDtypeStruct(right_side.shape, f32)
    return local(
        functools.partial(solve_kernel, LATE), (out, out, *state, parts), scratch,
        *fixed, *[inside(x) for x in kept], *edges[3:], inside(message), index, halo, basis,
        aliases={2: 2, 3: 3, 4: 4, 5: 5},
    )[:2]


def solution(mesh):
    return jax.shard_map(
        step,
        mesh=mesh,
        in_specs=(
            P(None, "blk", "nrm"),
            P(None, "blk", "nrm"),
            P(),
            P(None, "blk", "nrm"),
            P("blk", "nrm"),
            P("blk", "nrm"),
            P("blk", None, "nrm"),
        ),
        out_specs=(P(None, "blk", "nrm"), P(None, "blk", "nrm")),
        check_vma=False,
    )
```
